32 devices in a mesh: block: 4 (over y, x), dp: 8 (over z, core).
Axes of the slice: x: 2, y: 2, z: 4, core: 2. Of those that a mesh axis runs over, the one named last changes fastest.
Arguments:
- tokens: bfloat16 [2048, 16384], P('dp', 'block'), may hold values from -6 to 6
- first_up: bfloat16 [128, 128, 128], P('block'), may hold values from -0.5 to 0.5
- second_up: bfloat16 [128, 128, 512], P('block'), may hold values from -0.5 to 0.5
- first_down: bfloat16 [128, 512, 128], P('block'), may hold values from -0.25 to 0.25
- second_down: bfloat16 [128, 128, 128], P('block'), may hold values from -0.5 to 0.5
- cotangent: bfloat16 [2048, 16384], P('dp', 'block'), may hold values from -6 to 6
Outputs:
- output: bfloat16 [2048, 16384], P('dp', 'block')
- input_grad: bfloat16 [2048, 16384], P('dp', 'block')
- grad_first_up: float32 [128, 128, 128], P('block', 'dp')
- grad_second_up: float32 [128, 128, 512], P('block', 'dp')
- grad_first_down: float32 [128, 512, 128], P('block', 'dp')
- grad_second_down: float32 [128, 128, 128], P('block', 'dp')
The draws below stay inside these ranges and needn't reach their ends.
All inputs are finite; a program needn't handle non-finite values.
Results may differ from the reference program's by a relative error of at most 0.0071.
Values may be sent and summed in bfloat16 or wider, within the bound.
No kernel may reach another device: no remote copies, remote signals or barrier semaphores. Data moves between devices by JAX's collectives and lax.ppermute only.
A program may use at most 192 MiB of HBM per device.

```python
import math
import jax
import jax.numpy as jnp
from jax import lax

D = 16384
NB = 128
TOK_DEV = 256
BS = 128
HB = 512
TOKENS = 2048
N_DP = 8


def with_spikes(values, rng, source, target, parts, factor):
    owner, partner = [(jnp.arange(values.shape[axis_at]) // (values.shape[axis_at] // parts)).reshape([-1 if axis == axis_at else 1 for axis in range(values.ndim)]) for axis_at in (source, target)]
    chosen = jax.random.permutation(rng, parts)[partner]
    strong = (owner == chosen) | (owner == (partner + parts // 2) % parts)
    return jnp.where(strong, factor * values, values)


def levels(rng, extent, shards, low, top_value):
    level, own = 1.0, jax.random.fold_in(rng, 6)
    for position, blocks in shards:
        draws = jnp.exp(jax.random.uniform(jax.random.fold_in(own, position), (blocks,), jnp.float32, low / len(shards), top_value / len(shards)))
        level = level * jnp.repeat(draws, extent[position] // blocks).reshape([-1 if axis == position else 1 for axis in range(len(extent))])
    return level


def gaussian(key, extent, scale, reach, cuts=(), held_as=jnp.bfloat16):
    level = levels(key, extent, cuts, -0.22, 0.18) if cuts else 1.0
    array = jax.random.normal(key, extent, jnp.float32) * scale * level
    return jnp.minimum(jnp.maximum(array, -reach), reach).astype(held_as)


def noise_with(stream_key, dims, width, bound, cuts, heavy, held_as=jnp.bfloat16):
    array = width * jax.random.normal(stream_key, dims, jnp.float32)
    if cuts:
        array = array * levels(stream_key, dims, cuts, -0.22, 0.18)
    return jnp.clip(with_spikes(array, jax.random.fold_in(stream_key, 3), *heavy), -bound, bound).astype(held_as)


def setup_inputs(seed: int = 0) -> dict:
    arg_keys = jax.random.split(jax.random.key(seed), 7)
    return {
        "tokens": gaussian(arg_keys[0], (TOKENS, D), 1.0, 6.0, ((0, 8), (1, 4))),
        "first_up": gaussian(arg_keys[1], (NB, BS, BS), BS ** -0.5, 0.5, ((0, 4),)),
        "second_up": gaussian(arg_keys[2], (BS, NB, HB), NB ** -0.5, 0.5, ((0, 4),)),
        "first_down": gaussian(arg_keys[3], (BS, HB, NB), HB ** -0.5, 0.25, ((0, 4),)),
        "second_down": gaussian(arg_keys[4], (NB, BS, BS), BS ** -0.5, 0.5, ((0, 4),)),
        "cotangent": noise_with(arg_keys[5], (TOKENS, D), 1.0, 6.0, ((0, 8), (1, 4)), (0, 1, 8, 2.0)),
    }


def gelu_pair(values):
    factor = math.sqrt(2.0 / math.pi)
    tanh_part = jnp.tanh(factor * (values + 0.044715 * values * values * values))
    active = 0.5 * values * (1.0 + tanh_part)
    slope_term = 0.5 * (1.0 + tanh_part) + 0.5 * values * (1.0 - tanh_part * tanh_part) * factor * (1.0 + 3.0 * 0.044715 * values * values)
    return (active, slope_term)

def reference(tokens, first_up, second_up, first_down, second_down, cotangent):
    wide = jnp.float32
    narrow = jnp.bfloat16
    up_one = first_up.astype(wide)
    up_two = second_up.astype(wide)
    down_one = first_down.astype(wide)
    down_two = second_down.astype(wide)

    def one_block(totals, pieces):
        token_rows, cot_rows = pieces
        count = token_rows.shape[0]
        inputs_f = token_rows.reshape(count, NB, BS).astype(wide)
        cot_f = cot_rows.reshape(count, NB, BS).astype(wide)
        mixed_in = jnp.einsum('tbi,bij->tbj', inputs_f, up_one).astype(narrow)
        mixed_f = mixed_in.astype(wide)
        before = jnp.einsum('tbj,jbk->tjk', mixed_f, up_two)
        active, slope_term = gelu_pair(before)
        active_f = active.astype(narrow).astype(wide)
        mixed_out = jnp.einsum('tjk,jkb->tbj', active_f, down_one).astype(narrow)
        mixed_out_f = mixed_out.astype(wide)
        result = jnp.einsum('tbj,bji->tbi', mixed_out_f, down_two).astype(narrow)
        g_sd = jnp.einsum('tbj,tbi->bji', mixed_out_f, cot_f)
        back_out = jnp.einsum('tbi,bji->tbj', cot_f, down_two).astype(narrow).astype(wide)
        g_fd = jnp.einsum('tjk,tbj->jkb', active_f, back_out)
        back_pre = (jnp.einsum('tbj,jkb->tjk', back_out, down_one) * slope_term).astype(narrow).astype(wide)
        g_su = jnp.einsum('tbj,tjk->jbk', mixed_f, back_pre)
        back_in = jnp.einsum('tjk,jbk->tbj', back_pre, up_two).astype(narrow).astype(wide)
        g_fu = jnp.einsum('tbi,tbj->bij', inputs_f, back_in)
        input_rows = jnp.einsum('tbj,bij->tbi', back_in, up_one).astype(narrow)
        new_totals = (totals[0] + g_fu, totals[1] + g_su, totals[2] + g_fd, totals[3] + g_sd)
        return (new_totals, (result.reshape(count, D), input_rows.reshape(count, D)))
    start = (jnp.zeros((NB, BS, BS), jnp.float32), jnp.zeros((BS, NB, HB), jnp.float32), jnp.zeros((BS, HB, NB), jnp.float32), jnp.zeros((NB, BS, BS), jnp.float32))
    totals, (outputs, input_rows) = lax.scan(one_block, start, (tokens.reshape(N_DP, TOK_DEV, D), cotangent.reshape(N_DP, TOK_DEV, D)))
    return (outputs.reshape(TOKENS, D), input_rows.reshape(TOKENS, D), totals[0], totals[1], totals[2], totals[3])
```

```python
import functools
import math

import jax
import jax.numpy as jnp
from jax import lax
from jax.experimental import pallas as pl
from jax.experimental.pallas import tpu as pltpu
from jax.sharding import PartitionSpec as P

NARROW = jnp.bfloat16
WIDE = jnp.float32
LANES = 128
ROWS = 16
CHUNKS = 4
CORES = 2


def gelu_pair(values):
    factor = math.sqrt(2.0 / math.pi)
    square = values * values
    tanh_part = jnp.tanh(factor * values * (1.0 + 0.044715 * square))
    half = 0.5 + 0.5 * tanh_part
    active = values * half
    slope_term = half + active * (1.0 - tanh_part) * (factor + (3.0 * 0.044715 * factor) * square)
    return (active, slope_term)


def dot(a, b, ca, cb):
    return lax.dot_general(a, b, (((ca,), (cb,)), ((), ())), preferred_element_type=WIDE)


def spread(scr, b, width, rows, value):
    for h in range(scr.shape[0]):
        scr[h, pl.ds(b, width, stride=rows), :] = value[:, h * LANES : (h + 1) * LANES]


def collect(scr, b, width, rows):
    pieces = [scr[h, pl.ds(b, width, stride=rows), :] for h in range(scr.shape[0])]
    return jnp.concatenate(pieces, axis=1).astype(NARROW)


def mix_in_body(groups, chunks, sc_ref, x_ref, g_ref, fu_ref, sd_ref, *rest):
    outs, (scr_u, scr_d) = rest[:-2], rest[-2:]
    rows, width = fu_ref.shape[0], fu_ref.shape[1]
    me = sc_ref[0]
    feats = width // groups
    part = feats // chunks
    for b in range(rows):
        cols = slice(b * width, (b + 1) * width)
        spread(scr_u, b, width, rows, dot(fu_ref[b], x_ref[:, cols], 0, 1))
        spread(scr_d, b, width, rows, dot(sd_ref[b], g_ref[:, cols], 1, 1))
    for c in range(chunks):
        for s in range(groups):
            ref = outs[c * groups + s]
            off = pl.multiple_of(((me ^ s) * feats + c * part) * rows, ROWS)
            for k, scr in enumerate((scr_u, scr_d)):
                for h in range(scr.shape[0]):
                    value = scr[h, pl.ds(off, part * rows), :].astype(NARROW)
                    ref[k, :, :, h * LANES : (h + 1) * LANES] = value.reshape(part, rows, LANES)


def mix_in(scalars, tokens, cotangent, first_up, second_down, groups, chunks):
    count = tokens.shape[0]
    blocks, width = first_up.shape[:2]
    part = width // groups // chunks
    shape = jax.ShapeDtypeStruct((2, part, blocks, count), NARROW)
    flat = pl.BlockSpec((count, ROWS * width), lambda i, sc: (0, i))
    mats = pl.BlockSpec((ROWS, width, width), lambda i, sc: (i, 0, 0))
    out = pl.BlockSpec((2, part, ROWS, count), lambda i, sc: (0, 0, i, 0))
    n_out = chunks * groups
    res = pl.pallas_call(
        functools.partial(mix_in_body, groups, chunks),
        grid_spec=pltpu.PrefetchScalarGridSpec(
            num_scalar_prefetch=1,
            grid=(blocks // ROWS,),
            in_specs=[flat, flat, mats, mats],
            out_specs=[out] * n_out,
            scratch_shapes=[pltpu.VMEM((count // LANES, width * ROWS, LANES), WIDE)] * 2,
        ),
        out_shape=[shape] * n_out,
        cost_estimate=pl.CostEstimate(
            flops=4 * count * blocks * width * width, transcendentals=0, bytes_accessed=8 * count * blocks * width
        ),
        name="mix_in",
    )(scalars, tokens, cotangent, first_up, second_down)
    return [res[c * groups : (c + 1) * groups] for c in range(chunks)]


def feature_body(groups, line, sc_ref, *rest):
    ins, (wu_ref, wd_ref) = rest[:groups], rest[groups : groups + 2]
    outs = rest[groups + 2 : 2 * groups + 2]
    keep_ref, send_ref, u_scr, d_scr, v_scr, e_scr = rest[2 * groups + 2 :]
    me, core = sc_ref[0], sc_ref[2]
    blocks = ins[0].shape[2]
    for s in range(groups):
        off = pl.multiple_of((me ^ s) * blocks, ROWS)
        u_scr[pl.ds(off, blocks), :] = ins[s][0, 0]
        d_scr[pl.ds(off, blocks), :] = ins[s][1, 0]
    u, d = u_scr[...], d_scr[...]
    wu, wd = wu_ref[0], wd_ref[0]
    active, slope = gelu_pair(dot(wu, u, 0, 0))
    active = active.astype(NARROW)
    v_scr[...] = dot(wd, active, 0, 0).astype(NARROW)
    back = (dot(wd, d, 1, 0) * slope).astype(NARROW)
    e_scr[...] = dot(wu, back, 1, 0).astype(NARROW)
    for s in range(groups):
        off = pl.multiple_of((me ^ s) * blocks, ROWS)
        outs[s][0, 0] = v_scr[pl.ds(off, blocks), :]
        outs[s][1, 0] = e_scr[pl.ds(off, blocks), :]
    g_su = dot(u, back, 1, 1)
    g_fd = dot(active, d, 1, 1)
    r_su = g_su.shape[0] // (CORES * line)
    r_fd = g_fd.shape[0] // (CORES * line)
    fold = g_su.shape[1] // g_fd.shape[1]
    first = core == 0
    for p in range(line):
        halves = []
        for k in range(CORES):
            r = p * CORES + k
            block = g_fd[r * r_fd : (r + 1) * r_fd]
            step = r_fd // fold
            wide = jnp.concatenate([block[f * step : (f + 1) * step] for f in range(fold)], axis=1)
            halves.append(jnp.concatenate([g_su[r * r_su : (r + 1) * r_su], wide], axis=0))
        keep_ref[p, 0] = jnp.where(first, halves[0], halves[1]).astype(NARROW)
        send_ref[p, 0] = jnp.where(first, halves[1], halves[0]).astype(NARROW)


def feature(scalars, arrays, second_up, first_down, c, line):
    groups = len(arrays)
    _, part, blocks, count = arrays[0].shape
    width, hidden = second_up.shape[1:]
    r_su = width // (CORES * line)
    data = pl.BlockSpec((2, 1, blocks, count), lambda i, sc: (0, i, 0, 0))
    grads = pl.BlockSpec((line, 1, 2 * r_su, hidden), lambda i, sc: (0, i, 0, 0))
    g_shape = jax.ShapeDtypeStruct((line, part, 2 * r_su, hidden), NARROW)
    scr = pltpu.VMEM((groups * blocks, count), NARROW)
    res = pl.pallas_call(
        functools.partial(feature_body, groups, line),
        grid_spec=pltpu.PrefetchScalarGridSpec(
            num_scalar_prefetch=1,
            grid=(part,),
            in_specs=[data] * groups
            + [
                pl.BlockSpec((1, width, hidden), lambda i, sc: (c * part + i, 0, 0)),
                pl.BlockSpec((1, hidden, width), lambda i, sc: (c * part + i, 0, 0)),
            ],
            out_specs=[data] * groups + [grads] * 2,
            scratch_shapes=[scr] * 4,
        ),
        out_shape=[jax.ShapeDtypeStruct(arrays[0].shape, NARROW)] * groups + [g_shape] * 2,
        cost_estimate=pl.CostEstimate(
            flops=12 * part * count * width * hidden,
            transcendentals=part * count * hidden,
            bytes_accessed=part * (8 * width * hidden + 8 * count * width),
        ),
        name="feature",
    )(scalars, *arrays, second_up, first_down)
    return res[:groups], res[groups], res[groups + 1]


def mix_out_body(groups, chunks, line, sc_ref, *rest):
    n_in = chunks * groups
    ins = rest[:n_in]
    x_ref, g_ref, fu_ref, sd_ref, out_ref, ig_ref, keep_ref, send_ref, scr_v, scr_d = rest[n_in:]
    rows, width = fu_ref.shape[0], fu_ref.shape[1]
    me, core = sc_ref[0], sc_ref[2]
    feats = width // groups
    part = feats // chunks
    for c in range(chunks):
        for s in range(groups):
            ref = ins[c * groups + s]
            off = pl.multiple_of(((me ^ s) * feats + c * part) * rows, ROWS)
            for k, scr in enumerate((scr_v, scr_d)):
                for h in range(scr.shape[0]):
                    value = ref[k, :, :, h * LANES : (h + 1) * LANES]
                    scr[h, pl.ds(off, part * rows), :] = value.reshape(part * rows, LANES).astype(WIDE)
    first = core == 0
    r_one = width // (CORES * line)
    for b in range(rows):
        cols = slice(b * width, (b + 1) * width)
        v = collect(scr_v, b, width, rows)
        d = collect(scr_d, b, width, rows)
        out_ref[:, cols] = dot(v, sd_ref[b], 0, 0).astype(NARROW)
        ig_ref[:, cols] = dot(d, fu_ref[b], 0, 1).astype(NARROW)
        g_sd = dot(v, g_ref[:, cols], 1, 0)
        g_fu = dot(x_ref[:, cols], d, 0, 1)
        for p in range(line):
            halves = []
            for k in range(CORES):
                r = p * CORES + k
                own = slice(r * r_one, (r + 1) * r_one)
                halves.append(jnp.concatenate([g_fu[own], g_sd[own]], axis=0))
            keep_ref[p, b] = jnp.where(first, halves[0], halves[1]).astype(NARROW)
            send_ref[p, b] = jnp.where(first, halves[1], halves[0]).astype(NARROW)


def mix_out(scalars, arrays, tokens, cotangent, first_up, second_down, line):
    chunks, groups = len(arrays), len(arrays[0])
    _, part, blocks, count = arrays[0][0].shape
    width = first_up.shape[1]
    r_one = width // (CORES * line)
    data = pl.BlockSpec((2, part, ROWS, count), lambda i, sc: (0, 0, i, 0))
    flat = pl.BlockSpec((count, ROWS * width), lambda i, sc: (0, i))
    mats = pl.BlockSpec((ROWS, width, width), lambda i, sc: (i, 0, 0))
    grads = pl.BlockSpec((line, ROWS, 2 * r_one, width), lambda i, sc: (0, i, 0, 0))
    g_shape = jax.ShapeDtypeStruct((line, blocks, 2 * r_one, width), NARROW)
    flat_shape = jax.ShapeDtypeStruct(tokens.shape, NARROW)
    return pl.pallas_call(
        functools.partial(mix_out_body, groups, chunks, line),
        grid_spec=pltpu.PrefetchScalarGridSpec(
            num_scalar_prefetch=1,
            grid=(blocks // ROWS,),
            in_specs=[data] * (chunks * groups) + [flat, flat, mats, mats],
            out_specs=[flat, flat, grads, grads],
            scratch_shapes=[pltpu.VMEM((count // LANES, width * ROWS, LANES), WIDE)] * 2,
        ),
        out_shape=[flat_shape, flat_shape, g_shape, g_shape],
        cost_estimate=pl.CostEstimate(
            flops=8 * count * blocks * width * width, transcendentals=0, bytes_accessed=16 * count * blocks * width
        ),
        name="mix_out",
    )(scalars, *[a for chunk in arrays for a in chunk], tokens, cotangent, first_up, second_down)


def settle_body(fold, n_extra, sc_ref, keep_ref, recv_ref, right_ref, left_ref, *rest):
    first_ref, second_ref = rest[n_extra:]
    total = (
        keep_ref[0].astype(WIDE)
        + recv_ref[0].astype(WIDE)
        + right_ref[...].astype(WIDE)
        + left_ref[...].astype(WIDE)
    )
    half = total.shape[1] // 2
    first_ref[...] = total[:, :half]
    width = total.shape[2] // fold
    for f in range(fold):
        second_ref[:, f * half : (f + 1) * half, :] = total[:, half:, f * width : (f + 1) * width]


def settle(scalars, keep, recv, right, left, fold, c, chunks, before):
    _, part, rows, cols = keep.shape
    tile = math.gcd(part, 8)
    steps = part // tile
    here = pl.BlockSpec((1, tile, rows, cols), lambda i, sc: (sc[1], i, 0, 0))
    came = pl.BlockSpec((tile, rows, cols), lambda i, sc: (i, 0, 0))
    half = rows // 2
    shapes = (
        (part * chunks, half, cols),
        (part * chunks, half * fold, cols // fold),
    )
    extra = [pl.BlockSpec(memory_space=pl.ANY)] * len(before)
    return pl.pallas_call(
        functools.partial(settle_body, fold, len(before)),
        grid_spec=pltpu.PrefetchScalarGridSpec(
            num_scalar_prefetch=1,
            grid=(steps,),
            in_specs=[here, here, came, came] + extra,
            out_specs=[
                pl.BlockSpec((tile,) + s[1:], lambda i, sc: (c * steps + i, 0, 0)) for s in shapes
            ],
        ),
        out_shape=[jax.ShapeDtypeStruct(s, WIDE) for s in shapes],
        input_output_aliases={5 + k: k for k in range(len(before))},
        cost_estimate=pl.CostEstimate(
            flops=4 * part * rows * cols, transcendentals=0, bytes_accessed=12 * part * rows * cols
        ),
        name="settle",
    )(scalars, keep, recv, right, left, *before)


def line_sum(keep, send, place, line):
    swap = [(i, i ^ 1) for i in range(CORES * line)]
    recv = lax.ppermute(send, "dp", swap)
    to_right = [(i, i + CORES) for i in range(CORES * (line - 1))]
    to_left = [(i + CORES, i) for i in range(CORES * (line - 1))]

    def outgoing(target, carried):
        at = jnp.clip(target, 0, line - 1)
        total = lax.dynamic_index_in_dim(keep, at, 0, False).astype(WIDE) + lax.dynamic_index_in_dim(
            recv, at, 0, False
        ).astype(WIDE)
        if carried is not None:
            total = total + carried.astype(WIDE)
        return total.astype(NARROW)

    right = left = None
    for step in range(1, line):
        live = CORES * step
        out_r = outgoing(line - step + place, right)
        out_l = outgoing(place + step - line, left)
        right = lax.ppermute(out_r, "dp", to_right[:live])
        left = lax.ppermute(out_l, "dp", to_left[len(to_left) - live :])
    return recv, right, left


def local(tokens, first_up, second_up, first_down, second_down, cotangent):
    groups = lax.axis_size("block")
    line = lax.axis_size("dp") // CORES
    feats = second_up.shape[0]
    chunks = math.gcd(CHUNKS, feats)
    spot = lax.axis_index("dp").astype(jnp.int32)
    place = spot // CORES
    scalars = jnp.stack([lax.axis_index("block").astype(jnp.int32), place, spot % CORES])

    def exchange(arrays):
        return [arrays[0]] + [
            lax.ppermute(arrays[s], "block", [(i, i ^ s) for i in range(groups)]) for s in range(1, groups)
        ]

    packed = mix_in(scalars, tokens, cotangent, first_up, second_down, groups, chunks)
    packed = [exchange(a) for a in packed]
    fold = second_up.shape[2] // second_up.shape[1]
    backs, done = [], ()
    for c in range(chunks):
        back, keep, send = feature(scalars, packed[c], second_up, first_down, c, line)
        backs.append(exchange(back))
        recv, right, left = line_sum(keep, send, place, line)
        done = settle(scalars, keep, recv, right, left, fold, c, chunks, done)
    red_su, red_fd = done
    result, input_rows, keep, send = mix_out(
        scalars, backs, tokens, cotangent, first_up, second_down, line
    )
    recv, right, left = line_sum(keep, send, place, line)
    red_fu, red_sd = settle(scalars, keep, recv, right, left, 1, 0, 1, ())
    return (result, input_rows, red_fu, red_su, red_fd, red_sd)


def plain_local(tokens, first_up, second_up, first_down, second_down, cotangent):
    groups = lax.axis_size("block")
    blocks, width = first_up.shape[:2]
    feats = width // groups
    count = tokens.shape[0]
    x = tokens.reshape(count, blocks, width)
    g = cotangent.reshape(count, blocks, width)

    def mul(spec, a, b):
        return jnp.einsum(spec, a, b, preferred_element_type=WIDE)

    def to_feats(array):
        array = array.astype(NARROW).reshape(count, blocks, groups, feats).transpose(0, 2, 1, 3)
        array = lax.all_to_all(array, "block", split_axis=1, concat_axis=1, tiled=True)
        return array.reshape(count, -1, feats)

    def to_blocks(array):
        array = array.astype(NARROW).reshape(count, groups, blocks, feats)
        array = lax.all_to_all(array, "block", split_axis=1, concat_axis=1, tiled=True)
        return array.transpose(0, 2, 1, 3).reshape(count, blocks, width)

    u = to_feats(mul("tbi,bij->tbj", x, first_up))
    d = to_feats(mul("tbi,bji->tbj", g, second_down))
    active, slope = gelu_pair(mul("tbj,jbk->tjk", u, second_up))
    active = active.astype(NARROW)
    v = to_blocks(mul("tjk,jkb->tbj", active, first_down))
    back = (mul("tbj,jkb->tjk", d, first_down) * slope).astype(NARROW)
    e = to_blocks(mul("tjk,jbk->tbj", back, second_up))
    grads = (
        mul("tbi,tbj->bij", x, e),
        mul("tbj,tjk->jbk", u, back),
        mul("tjk,tbj->jkb", active, d),
        mul("tbj,tbi->bji", v, g),
    )
    result = mul("tbj,bji->tbi", v, second_down).astype(NARROW)
    input_rows = mul("tbj,bij->tbi", e, first_up).astype(NARROW)
    reduced = tuple(lax.psum_scatter(a, "dp", scatter_dimension=1, tiled=True) for a in grads)
    return (result.reshape(count, -1), input_rows.reshape(count, -1)) + reduced


def solution(mesh):
    placed = (
        P("dp", "block"),
        P("block", None, None),
        P("block", None, None),
        P("block", None, None),
        P("block", None, None),
        P("dp", "block"),
    )
    groups, n_dp = mesh.shape["block"], mesh.shape["dp"]

    def body(tokens, first_up, second_up, first_down, second_down, cotangent):
        blocks, width = first_up.shape[:2]
        hidden = second_up.shape[2]
        fits = (
            groups & (groups - 1) == 0
            and n_dp % CORES == 0
            and n_dp > CORES
            and blocks % ROWS == 0
            and width % LANES == 0
            and hidden % width == 0
            and width % (n_dp * ROWS) == 0
            and tokens.shape[0] % LANES == 0
        )
        run = local if fits else plain_local
        return run(tokens, first_up, second_up, first_down, second_down, cotangent)

    return jax.shard_map(
        body,
        mesh=mesh,
        in_specs=placed,
        out_specs=(
            P("dp", "block"),
            P("dp", "block"),
            P("block", "dp", None),
            P("block", "dp", None),
            P("block", "dp", None),
            P("block", "dp", None),
        ),
        check_vma=False,
    )
```

```python
import functools
import math

import jax
import jax.numpy as jnp
from jax import lax
from jax.experimental import pallas as pl
from jax.experimental.pallas import tpu as pltpu
from jax.sharding import PartitionSpec as P


NARROW = jnp.bfloat16
WIDE = jnp.float32
LANES = 128
ROWS = 16
PITCH = 24
CHUNKS = 4
STEP = 4
CORES = 2


def gelu_pair(values):
    factor = math.sqrt(2.0 / math.pi)
    square = values * values
    tanh_part = jnp.tanh(factor * values * (1.0 + 0.044715 * square))
    half = 0.5 + 0.5 * tanh_part
    active = values * half
    slope_term = half + active * (1.0 - tanh_part) * (factor + (3.0 * 0.044715 * factor) * square)
    return (active, slope_term)


def dot(a, b, ca, cb):
    return lax.dot_general(a, b, (((ca,), (cb,)), ((), ())), preferred_element_type=WIDE)


def spread(scr, b, width, value):
    for h in range(scr.shape[0]):
        scr[h, pl.ds(b, width, stride=PITCH), :] = value[:, h * LANES : (h + 1) * LANES]


def collect(scr, b, width):
    pieces = [scr[h, pl.ds(b, width, stride=PITCH), :] for h in range(scr.shape[0])]
    return jnp.concatenate(pieces, axis=1).astype(NARROW)


def mix_in_body(groups, chunks, x_ref, g_ref, fu_ref, sd_ref, *rest):
    outs, (scr_u, scr_d) = rest[:-2], rest[-2:]
    rows, width = fu_ref.shape[0], fu_ref.shape[1]
    me = lax.axis_index("block")
    feats = width // groups
    part = feats // chunks
    for b in range(rows):
        cols = slice(b * width, (b + 1) * width)
        spread(scr_u, b, width, dot(fu_ref[b], x_ref[:, cols], 0, 1))
        spread(scr_d, b, width, dot(sd_ref[b], g_ref[:, cols], 1, 1))
    for c in range(chunks):
        for s in range(groups):
            ref = outs[c * groups + s]
            off = pl.multiple_of(((me ^ s) * feats + c * part) * PITCH, 8)
            for k, scr in enumerate((scr_u, scr_d)):
                for h in range(scr.shape[0]):
                    for n in range(part):
                        value = scr[h, pl.ds(off + n * PITCH, rows), :]
                        ref[k, n, :, h * LANES : (h + 1) * LANES] = value.astype(NARROW)


def mix_in(tokens, cotangent, first_up, second_down, groups, chunks):
    count = tokens.shape[0]
    blocks, width = first_up.shape[:2]
    part = width // groups // chunks
    shape = jax.ShapeDtypeStruct((2, part, blocks, count), NARROW)
    flat = pl.BlockSpec((count, ROWS * width), lambda i: (0, i))
    mats = pl.BlockSpec((ROWS, width, width), lambda i: (i, 0, 0))
    out = pl.BlockSpec((2, part, ROWS, count), lambda i: (0, 0, i, 0))
    n_out = chunks * groups
    res = pl.pallas_call(
        functools.partial(mix_in_body, groups, chunks),
        grid=(blocks // ROWS,),
        in_specs=[flat, flat, mats, mats],
        out_specs=[out] * n_out,
        scratch_shapes=[pltpu.VMEM((count // LANES, width * PITCH, LANES), WIDE)] * 2,
        out_shape=[shape] * n_out,
        cost_estimate=pl.CostEstimate(
            flops=4 * count * blocks * width * width, transcendentals=0, bytes_accessed=8 * count * blocks * width
        ),
        name="mix_in",
    )(tokens, cotangent, first_up, second_down)
    return [res[c * groups : (c + 1) * groups] for c in range(chunks)]


def mirrored(value, bits):
    return sum(((value >> t) & 1) << (bits - 1 - t) for t in range(bits))


def feature_body(groups, line, *rest):
    ins, (wu_ref, wd_ref) = rest[:groups], rest[groups : groups + 2]
    outs = rest[groups + 2 : 2 * groups + 2]
    keep_ref, send_ref, u_scr, d_scr, v_scr, e_scr = rest[2 * groups + 2 :]
    me = lax.axis_index("block")
    first = lax.axis_index("dp") % CORES == 0
    blocks = ins[0].shape[2]
    offs = [pl.multiple_of((me ^ s) * blocks, ROWS) for s in range(groups)]
    bits = line.bit_length() - 1
    for n in range(wu_ref.shape[0]):
        for s in range(groups):
            u_scr[n, pl.ds(offs[s], blocks), :] = ins[s][0, n]
            d_scr[n, pl.ds(offs[s], blocks), :] = ins[s][1, n]
    for n in range(wu_ref.shape[0]):
        u, d = u_scr[n], d_scr[n]
        wu, wd = wu_ref[n], wd_ref[n]
        active, slope = gelu_pair(dot(wu, u, 0, 0))
        active = active.astype(NARROW)
        v_scr[n] = dot(wd, active, 0, 0).astype(NARROW)
        back = (dot(wd, d, 1, 0) * slope).astype(NARROW)
        e_scr[n] = dot(wu, back, 1, 0).astype(NARROW)
        g_su = dot(u, back, 1, 1)
        g_fd = dot(active, d, 1, 1)
        r_su = g_su.shape[0] // (CORES * line)
        r_fd = g_fd.shape[0] // (CORES * line)
        fold = g_su.shape[1] // g_fd.shape[1]
        step = r_fd // fold
        for p in range(line):
            at = mirrored(p, bits)
            halves = []
            for k in range(CORES):
                r = p * CORES + k
                block = g_fd[r * r_fd : (r + 1) * r_fd]
                wide = jnp.concatenate([block[f * step : (f + 1) * step] for f in range(fold)], axis=1)
                halves.append((g_su[r * r_su : (r + 1) * r_su], wide))
            for h in range(2):
                rows = slice(h * r_su, (h + 1) * r_su)
                keep_ref[at, n, rows, :] = jnp.where(first, halves[0][h], halves[1][h]).astype(NARROW)
                send_ref[at, n, rows, :] = jnp.where(first, halves[1][h], halves[0][h]).astype(NARROW)
    for n in range(wu_ref.shape[0]):
        for s in range(groups):
            outs[s][0, n] = v_scr[n, pl.ds(offs[s], blocks), :]
            outs[s][1, n] = e_scr[n, pl.ds(offs[s], blocks), :]


def feature(arrays, second_up, first_down, c, line):
    groups = len(arrays)
    _, part, blocks, count = arrays[0].shape
    width, hidden = second_up.shape[1:]
    r_su = width // (CORES * line)
    each = math.gcd(STEP, part)
    steps = part // each
    data = pl.BlockSpec((2, each, blocks, count), lambda i: (0, i, 0, 0))
    grads = pl.BlockSpec((line, each, 2 * r_su, hidden), lambda i: (0, i, 0, 0))
    g_shape = jax.ShapeDtypeStruct((line, part, 2 * r_su, hidden), NARROW)
    scr = pltpu.VMEM((each, groups * blocks, count), NARROW)
    res = pl.pallas_call(
        functools.partial(feature_body, groups, line),
        grid=(steps,),
        in_specs=[data] * groups
        + [
            pl.BlockSpec((each, width, hidden), lambda i: (c * steps + i, 0, 0)),
            pl.BlockSpec((each, hidden, width), lambda i: (c * steps + i, 0, 0)),
        ],
        out_specs=[data] * groups + [grads] * 2,
        scratch_shapes=[scr] * 4,
        out_shape=[jax.ShapeDtypeStruct(arrays[0].shape, NARROW)] * groups + [g_shape] * 2,
        cost_estimate=pl.CostEstimate(
            flops=12 * part * count * width * hidden,
            transcendentals=part * count * hidden,
            bytes_accessed=part * (8 * width * hidden + 8 * count * width),
        ),
        name="feature",
    )(*arrays, second_up, first_down)
    return res[:groups], res[groups], res[groups + 1]


def mix_out_body(groups, chunks, line, *rest):
    n_in = chunks * groups
    ins = rest[:n_in]
    x_ref, g_ref, fu_ref, sd_ref, out_ref, ig_ref, keep_ref, send_ref, scr_v, scr_d = rest[n_in:]
    rows, width = fu_ref.shape[0], fu_ref.shape[1]
    me = lax.axis_index("block")
    bits = line.bit_length() - 1
    feats = width // groups
    part = feats // chunks
    for c in range(chunks):
        for s in range(groups):
            ref = ins[c * groups + s]
            off = pl.multiple_of(((me ^ s) * feats + c * part) * PITCH, 8)
            for k, scr in enumerate((scr_v, scr_d)):
                for h in range(scr.shape[0]):
                    for n in range(part):
                        value = ref[k, n, :, h * LANES : (h + 1) * LANES]
                        scr[h, pl.ds(off + n * PITCH, rows), :] = value.astype(WIDE)
    first = lax.axis_index("dp") % CORES == 0
    r_one = width // (CORES * line)
    for b in range(rows):
        cols = slice(b * width, (b + 1) * width)
        v = collect(scr_v, b, width)
        d = collect(scr_d, b, width)
        out_ref[:, cols] = dot(v, sd_ref[b], 0, 0).astype(NARROW)
        ig_ref[:, cols] = dot(d, fu_ref[b], 0, 1).astype(NARROW)
        g_sd = dot(v, g_ref[:, cols], 1, 0)
        g_fu = dot(x_ref[:, cols], d, 0, 1)
        for p in range(line):
            halves = []
            for k in range(CORES):
                r = p * CORES + k
                own = slice(r * r_one, (r + 1) * r_one)
                halves.append(jnp.concatenate([g_fu[own], g_sd[own]], axis=0))
            at = mirrored(p, bits)
            keep_ref[at, b] = jnp.where(first, halves[0], halves[1]).astype(NARROW)
            send_ref[at, b] = jnp.where(first, halves[1], halves[0]).astype(NARROW)


def mix_out(arrays, tokens, cotangent, first_up, second_down, line):
    chunks, groups = len(arrays), len(arrays[0])
    _, part, blocks, count = arrays[0][0].shape
    width = first_up.shape[1]
    r_one = width // (CORES * line)
    data = pl.BlockSpec((2, part, ROWS, count), lambda i: (0, 0, i, 0))
    flat = pl.BlockSpec((count, ROWS * width), lambda i: (0, i))
    mats = pl.BlockSpec((ROWS, width, width), lambda i: (i, 0, 0))
    grads = pl.BlockSpec((line, ROWS, 2 * r_one, width), lambda i: (0, i, 0, 0))
    g_shape = jax.ShapeDtypeStruct((line, blocks, 2 * r_one, width), NARROW)
    flat_shape = jax.ShapeDtypeStruct(tokens.shape, NARROW)
    return pl.pallas_call(
        functools.partial(mix_out_body, groups, chunks, line),
        grid=(blocks // ROWS,),
        in_specs=[data] * (chunks * groups) + [flat, flat, mats, mats],
        out_specs=[flat, flat, grads, grads],
        scratch_shapes=[pltpu.VMEM((count // LANES, width * PITCH, LANES), WIDE)] * 2,
        out_shape=[flat_shape, flat_shape, g_shape, g_shape],
        cost_estimate=pl.CostEstimate(
            flops=8 * count * blocks * width * width, transcendentals=0, bytes_accessed=16 * count * blocks * width
        ),
        name="mix_out",
    )(*[a for chunk in arrays for a in chunk], tokens, cotangent, first_up, second_down)


def settle_body(fold, n_sum, *rest):
    ins, (first_ref, second_ref) = rest[:n_sum], rest[-2:]
    total = ins[0][0].astype(WIDE)
    for ref in ins[1:]:
        total = total + ref[0].astype(WIDE)
    half = total.shape[1] // 2
    first_ref[...] = total[:, :half]
    width = total.shape[2] // fold
    for f in range(fold):
        second_ref[:, f * half : (f + 1) * half, :] = total[:, half:, f * width : (f + 1) * width]


def settle(parts, line, fold, c, chunks, before):
    _, part, rows, cols = parts[0].shape
    steps = math.gcd(part, 4)
    tile = part // steps
    bits = line.bit_length() - 1

    def spec(array):
        size = array.shape[0]

        def where(i):
            return (mirrored(lax.axis_index("dp") // CORES, bits) % size, i, 0, 0)

        return pl.BlockSpec((1, tile, rows, cols), where)

    half = rows // 2
    shapes = (
        (part * chunks, half, cols),
        (part * chunks, half * fold, cols // fold),
    )
    return pl.pallas_call(
        functools.partial(settle_body, fold, len(parts)),
        grid=(steps,),
        in_specs=[spec(a) for a in parts] + [pl.BlockSpec(memory_space=pl.ANY)] * len(before),
        out_specs=[pl.BlockSpec((tile,) + s[1:], lambda i: (c * steps + i, 0, 0)) for s in shapes],
        out_shape=[jax.ShapeDtypeStruct(s, WIDE) for s in shapes],
        input_output_aliases={len(parts) + k: k for k in range(len(before))},
        cost_estimate=pl.CostEstimate(
            flops=4 * part * rows * cols, transcendentals=0, bytes_accessed=12 * part * rows * cols
        ),
        name="settle",
    )(*parts, *before)


def line_sum(keep, send, line):
    recv = lax.ppermute(send, "dp", [(i, i ^ 1) for i in range(CORES * line)])
    parts = [keep, recv]
    bits = line.bit_length() - 1
    place = lax.axis_index("dp") // CORES
    spot = mirrored(place, bits)
    for t in range(bits):
        span = line >> t
        half = span // 2
        start = (spot // span) * span + (1 - ((place >> t) & 1)) * half
        total = sum(
            lax.dynamic_slice_in_dim(a, start % a.shape[0], half, 0).astype(WIDE) for a in parts
        ).astype(NARROW)
        hop = CORES << t
        parts.append(lax.ppermute(total, "dp", [(i, i ^ hop) for i in range(CORES * line)]))
    return parts


def local(tokens, first_up, second_up, first_down, second_down, cotangent):
    groups = lax.axis_size("block")
    line = lax.axis_size("dp") // CORES
    chunks = math.gcd(CHUNKS, second_up.shape[0])

    def exchange(arrays):
        got = [arrays[0]]
        for s in range(1, groups):
            got.append(lax.ppermute(arrays[s], "block", [(i, i ^ s) for i in range(groups)]))
        return got

    packed = mix_in(tokens, cotangent, first_up, second_down, groups, chunks)
    packed = [exchange(a) for a in packed]
    fold = second_up.shape[2] // second_up.shape[1]
    backs, done = [], ()
    for c in range(chunks):
        back, keep, send = feature(packed[c], second_up, first_down, c, line)
        backs.append(exchange(back))
        parts = line_sum(keep, send, line)
        done = settle(parts, line, fold, c, chunks, done)
    red_su, red_fd = done
    result, input_rows, keep, send = mix_out(backs, tokens, cotangent, first_up, second_down, line)
    parts = line_sum(keep, send, line)
    red_fu, red_sd = settle(parts, line, 1, 0, 1, ())
    return (result, input_rows, red_fu, red_su, red_fd, red_sd)


def plain_local(tokens, first_up, second_up, first_down, second_down, cotangent):
    groups = lax.axis_size("block")
    blocks, width = first_up.shape[:2]
    feats = width // groups
    count = tokens.shape[0]
    x = tokens.reshape(count, blocks, width)
    g = cotangent.reshape(count, blocks, width)

    def mul(spec, a, b):
        return jnp.einsum(spec, a, b, preferred_element_type=WIDE)

    def to_feats(array):
        array = array.astype(NARROW).reshape(count, blocks, groups, feats).transpose(0, 2, 1, 3)
        array = lax.all_to_all(array, "block", split_axis=1, concat_axis=1, tiled=True)
        return array.reshape(count, -1, feats)

    def to_blocks(array):
        array = array.astype(NARROW).reshape(count, groups, blocks, feats)
        array = lax.all_to_all(array, "block", split_axis=1, concat_axis=1, tiled=True)
        return array.transpose(0, 2, 1, 3).reshape(count, blocks, width)

    u = to_feats(mul("tbi,bij->tbj", x, first_up))
    d = to_feats(mul("tbi,bji->tbj", g, second_down))
    active, slope = gelu_pair(mul("tbj,jbk->tjk", u, second_up))
    active = active.astype(NARROW)
    v = to_blocks(mul("tjk,jkb->tbj", active, first_down))
    back = (mul("tbj,jkb->tjk", d, first_down) * slope).astype(NARROW)
    e = to_blocks(mul("tjk,jbk->tbj", back, second_up))
    grads = (
        mul("tbi,tbj->bij", x, e),
        mul("tbj,tjk->jbk", u, back),
        mul("tjk,tbj->jkb", active, d),
        mul("tbj,tbi->bji", v, g),
    )
    result = mul("tbj,bji->tbi", v, second_down).astype(NARROW)
    input_rows = mul("tbj,bij->tbi", e, first_up).astype(NARROW)
    reduced = tuple(lax.psum_scatter(a, "dp", scatter_dimension=1, tiled=True) for a in grads)
    return (result.reshape(count, -1), input_rows.reshape(count, -1)) + reduced


def solution(mesh):
    placed = (
        P("dp", "block"),
        P("block", None, None),
        P("block", None, None),
        P("block", None, None),
        P("block", None, None),
        P("dp", "block"),
    )
    groups, n_dp = mesh.shape["block"], mesh.shape["dp"]
    line = n_dp // CORES

    def suits(first_up, second_up, tokens):
        blocks, width, _ = first_up.shape
        blocks = blocks // groups
        hidden = second_up.shape[2]
        return (
            groups & (groups - 1) == 0
            and n_dp % CORES == 0
            and line > 1
            and line & (line - 1) == 0
            and blocks % ROWS == 0
            and width % LANES == 0
            and hidden % width == 0
            and width % (n_dp * ROWS) == 0
            and tokens.shape[0] // n_dp % LANES == 0
        )

    def step(tokens, first_up, second_up, first_down, second_down, cotangent):
        fits = suits(first_up, second_up, tokens)

        def body(*args):
            return (local if fits else plain_local)(*args)

        run = jax.shard_map(
            body,
            mesh=mesh,
            in_specs=placed,
            out_specs=(
                P("dp", "block"),
                P("dp", "block"),
                P("block", "dp", None),
                P("block", "dp", None),
                P("block", "dp", None),
                P("block", "dp", None),
            ),
            check_vma=False,
        )
        return run(tokens, first_up, second_up, first_down, second_down, cotangent)

    return step
```

```python
import functools
import math

import jax
import jax.numpy as jnp
from jax import lax
from jax.experimental import pallas as pl
from jax.experimental.pallas import tpu as pltpu
from jax.sharding import PartitionSpec as P


NARROW = jnp.bfloat16
WIDE = jnp.float32
LANES = 128
ROWS = 16
PITCH = 24
SHARES = (2, 2, 2, 2)
TILE = 128
MIB = 1 << 20
STEP = 4
CORES = 2


def gelu_pair(values):
    factor = math.sqrt(2.0 / math.pi)
    square = values * values
    tanh_part = jnp.tanh(factor * values * (1.0 + 0.044715 * square))
    half = 0.5 + 0.5 * tanh_part
    active = values * half
    slope_term = half + active * (1.0 - tanh_part) * (factor + (3.0 * 0.044715 * factor) * square)
    return (active, slope_term)


def dot(a, b, ca, cb):
    return lax.dot_general(a, b, (((ca,), (cb,)), ((), ())), preferred_element_type=WIDE)


def spread(scr, b, width, value):
    for h in range(scr.shape[0]):
        scr[h, pl.ds(b, width, stride=PITCH), :] = value[:, h * LANES : (h + 1) * LANES]


def split(feats):
    unit, rest = divmod(feats, sum(SHARES))
    sizes = [feats] if rest else [unit * share for share in SHARES]
    return [(size, sum(sizes[:c])) for c, size in enumerate(sizes)]


def mix_in_body(groups, x_ref, g_ref, fu_ref, sd_ref, *rest):
    outs, (scr_u, scr_d) = rest[:-2], rest[-2:]
    rows, width = fu_ref.shape[0], fu_ref.shape[1]
    me = lax.axis_index("block")
    feats = width // groups
    for b in range(rows):
        cols = slice(b * width, (b + 1) * width)
        spread(scr_u, b, width, dot(fu_ref[b], x_ref[:, cols], 0, 1))
        spread(scr_d, b, width, dot(sd_ref[b], g_ref[:, cols], 1, 1))
    for c, (part, begin) in enumerate(split(feats)):
        for s in range(groups):
            ref = outs[c * groups + s]
            off = pl.multiple_of(((me ^ s) * feats + begin) * PITCH, 8)
            for k, scr in enumerate((scr_u, scr_d)):
                for h in range(scr.shape[0]):
                    for n in range(part):
                        value = scr[h, pl.ds(off + n * PITCH, rows), :]
                        ref[k, n, :, h * LANES : (h + 1) * LANES] = value.astype(NARROW)


def mix_in(tokens, cotangent, first_up, second_down, groups):
    count = tokens.shape[0]
    blocks, width = first_up.shape[:2]
    parts = [size for size, _ in split(width // groups)]
    flat = pl.BlockSpec((count, ROWS * width), lambda i: (0, i))
    mats = pl.BlockSpec((ROWS, width, width), lambda i: (i, 0, 0))
    outs = [pl.BlockSpec((2, n, ROWS, count), lambda i: (0, 0, i, 0)) for n in parts for _ in range(groups)]
    res = pl.pallas_call(
        functools.partial(mix_in_body, groups),
        grid=(blocks // ROWS,),
        in_specs=[flat, flat, mats, mats],
        out_specs=outs,
        scratch_shapes=[pltpu.VMEM((count // LANES, width * PITCH, LANES), WIDE)] * 2,
        out_shape=[
            jax.ShapeDtypeStruct((2, n, blocks, count), NARROW) for n in parts for _ in range(groups)
        ],
        cost_estimate=pl.CostEstimate(
            flops=4 * count * blocks * width * width, transcendentals=0, bytes_accessed=8 * count * blocks * width
        ),
        compiler_params=pltpu.CompilerParams(vmem_limit_bytes=24 * MIB),
        name="mix_in",
    )(tokens, cotangent, first_up, second_down)
    return [res[c * groups : (c + 1) * groups] for c in range(len(parts))]


def mirrored(value, bits):
    return sum(((value >> t) & 1) << (bits - 1 - t) for t in range(bits))


def line_slots(line):
    bits = line.bit_length() - 1
    own = mirrored(lax.axis_index("dp") // CORES, bits)
    return [own ^ mirrored(p, bits) for p in range(line)]


def feature_body(groups, line, *rest):
    ins, (wu_ref, wd_ref) = rest[:groups], rest[groups : groups + 2]
    outs = rest[groups + 2 : -8]
    keep_ref, send_ref, u_scr, d_scr, v_scr, e_scr, a_scr, b_scr = rest[-8:]
    me = lax.axis_index("block")
    first = lax.axis_index("dp") % CORES == 0
    blocks = ins[0].shape[2]
    offs = [pl.multiple_of((me ^ s) * blocks, ROWS) for s in range(groups)]
    slots = line_slots(line)
    for n in range(wu_ref.shape[0]):
        for s in range(groups):
            u_scr[n, pl.ds(offs[s], blocks), :] = ins[s][0, n]
            d_scr[n, pl.ds(offs[s], blocks), :] = ins[s][1, n]
    hidden = wd_ref.shape[1]
    for n in range(wu_ref.shape[0]):
        u, d = u_scr[n], d_scr[n]
        for k in range(0, hidden, TILE):
            tile = slice(k, k + TILE)
            active, slope = gelu_pair(dot(wu_ref[n, :, tile], u, 0, 0))
            a_scr[n, tile, :] = active.astype(NARROW)
            b_scr[n, tile, :] = (dot(wd_ref[n, tile, :], d, 1, 0) * slope).astype(NARROW)
    for n in range(wu_ref.shape[0]):
        u, d = u_scr[n], d_scr[n]
        active, back = a_scr[n], b_scr[n]
        v_scr[n] = dot(wd_ref[n], active, 0, 0).astype(NARROW)
        e_scr[n] = dot(wu_ref[n], back, 1, 0).astype(NARROW)
        g_su = dot(u, back, 1, 1).astype(NARROW)
        g_fd = dot(active, d, 1, 1).astype(NARROW)
        r_su = g_su.shape[0] // (CORES * line)
        r_fd = g_fd.shape[0] // (CORES * line)
        fold = g_su.shape[1] // g_fd.shape[1]
        step = r_fd // fold
        for p, at in enumerate(slots):
            halves = []
            for k in range(CORES):
                r = p * CORES + k
                block = g_fd[r * r_fd : (r + 1) * r_fd]
                wide = jnp.concatenate([block[f * step : (f + 1) * step] for f in range(fold)], axis=1)
                halves.append((g_su[r * r_su : (r + 1) * r_su], wide))
            for h in range(2):
                rows = slice(h * r_su, (h + 1) * r_su)
                keep_ref[at, n, rows, :] = jnp.where(first, halves[0][h], halves[1][h])
                send_ref[at, n, rows, :] = jnp.where(first, halves[1][h], halves[0][h])
    for n in range(wu_ref.shape[0]):
        for s in range(groups):
            outs[s][0, n] = v_scr[n, pl.ds(offs[s], blocks), :]
            outs[len(outs) - groups + s][outs[0].shape[0] - 1, n] = e_scr[n, pl.ds(offs[s], blocks), :]


def feature(arrays, second_up, first_down, begin, joint, line):
    groups = len(arrays)
    _, part, blocks, count = arrays[0].shape
    width, hidden = second_up.shape[1:]
    r_su = width // (CORES * line)
    each = math.gcd(STEP, part, begin)
    first = begin // each
    steps = part // each
    kinds = 2 if joint else 1
    n_out = 2 * groups // kinds
    back = pl.BlockSpec((kinds, each, blocks, count), lambda i: (0, i, 0, 0))
    data = pl.BlockSpec((2, each, blocks, count), lambda i: (0, i, 0, 0))
    grads = pl.BlockSpec((line, each, 2 * r_su, hidden), lambda i: (0, i, 0, 0))
    g_shape = jax.ShapeDtypeStruct((line, part, 2 * r_su, hidden), NARROW)
    scr = pltpu.VMEM((each, groups * blocks, count), NARROW)
    res = pl.pallas_call(
        functools.partial(feature_body, groups, line),
        grid=(steps,),
        in_specs=[data] * groups
        + [
            pl.BlockSpec((each, width, hidden), lambda i: (first + i, 0, 0)),
            pl.BlockSpec((each, hidden, width), lambda i: (first + i, 0, 0)),
        ],
        out_specs=[back] * n_out + [grads] * 2,
        scratch_shapes=[scr] * 4 + [pltpu.VMEM((each, hidden, count), NARROW)] * 2,
        out_shape=[jax.ShapeDtypeStruct((kinds, part, blocks, count), NARROW)] * n_out + [g_shape] * 2,
        cost_estimate=pl.CostEstimate(
            flops=12 * part * count * width * hidden,
            transcendentals=part * count * hidden,
            bytes_accessed=part * (8 * width * hidden + 8 * count * width),
        ),
        compiler_params=pltpu.CompilerParams(vmem_limit_bytes=20 * MIB),
        name="feature",
    )(*arrays, second_up, first_down)
    return res[:-2], res[-2], res[-1]


def mix_out_body(groups, line, to_output, *rest):
    ins = rest[:-6]
    flat_ref, mats_ref, out_ref, keep_ref, send_ref, scr = rest[-6:]
    rows, width = mats_ref.shape[0], mats_ref.shape[1]
    me = lax.axis_index("block")
    first = lax.axis_index("dp") % CORES == 0
    slots = line_slots(line)
    feats = width // groups
    for c, (part, begin) in enumerate(split(feats)):
        for s in range(groups):
            ref = ins[c * groups + s]
            off = pl.multiple_of(((me ^ s) * feats + begin) * PITCH, 8)
            for h in range(scr.shape[0]):
                for n in range(part):
                    value = ref[0, n, :, h * LANES : (h + 1) * LANES]
                    scr[h, pl.ds(off + n * PITCH, rows), :] = value.astype(WIDE)
    r_one = width // (CORES * line)
    for b in range(rows):
        cols = slice(b * width, (b + 1) * width)
        pieces = [scr[h, pl.ds(b, width, stride=PITCH), :] for h in range(scr.shape[0])]
        y = jnp.concatenate(pieces, axis=1).astype(NARROW)
        if to_output:
            out_ref[:, cols] = dot(y, mats_ref[b], 0, 0).astype(NARROW)
            grad = dot(y, flat_ref[:, cols], 1, 0).astype(NARROW)
        else:
            out_ref[:, cols] = dot(y, mats_ref[b], 0, 1).astype(NARROW)
            grad = dot(flat_ref[:, cols], y, 0, 1).astype(NARROW)
        for p, at in enumerate(slots):
            halves = [grad[(p * CORES + k) * r_one : (p * CORES + k + 1) * r_one] for k in range(CORES)]
            keep_ref[at, b] = jnp.where(first, halves[0], halves[1])
            send_ref[at, b] = jnp.where(first, halves[1], halves[0])


def mix_out(arrays, flat_in, mats_in, to_output, line):
    groups = len(arrays[0])
    blocks, width = mats_in.shape[:2]
    count = flat_in.shape[0]
    r_one = width // (CORES * line)

    def data(array):
        kind = 0 if to_output or array.shape[0] == 1 else 1
        return pl.BlockSpec((1, array.shape[1], ROWS, count), lambda i: (kind, 0, i, 0))

    flat = pl.BlockSpec((count, ROWS * width), lambda i: (0, i))
    mats = pl.BlockSpec((ROWS, width, width), lambda i: (i, 0, 0))
    grads = pl.BlockSpec((line, ROWS, r_one, width), lambda i: (0, i, 0, 0))
    g_shape = jax.ShapeDtypeStruct((line, blocks, r_one, width), NARROW)
    pieces = [a for chunk in arrays for a in chunk]
    return pl.pallas_call(
        functools.partial(mix_out_body, groups, line, to_output),
        grid=(blocks // ROWS,),
        in_specs=[data(a) for a in pieces] + [flat, mats],
        out_specs=[flat, grads, grads],
        scratch_shapes=[pltpu.VMEM((count // LANES, width * PITCH, LANES), WIDE)],
        out_shape=[jax.ShapeDtypeStruct(flat_in.shape, NARROW), g_shape, g_shape],
        cost_estimate=pl.CostEstimate(
            flops=4 * count * blocks * width * width, transcendentals=0, bytes_accessed=8 * count * blocks * width
        ),
        compiler_params=pltpu.CompilerParams(vmem_limit_bytes=18 * MIB),
        name="mix_out",
    )(*pieces, flat_in, mats_in)


def settle_body(fold, n_sum, *rest):
    ins, first_ref = rest[:n_sum], rest[-2 if fold else -1]
    total = ins[0][0].astype(WIDE)
    for ref in ins[1:]:
        total = total + ref[0].astype(WIDE)
    half = first_ref.shape[1]
    first_ref[...] = total[:, :half]
    for f in range(fold):
        second_ref = rest[-1]
        width = second_ref.shape[2]
        second_ref[:, f * half : (f + 1) * half, :] = total[:, half:, f * width : (f + 1) * width]


def settle(parts, fold, begin, feats, before):
    _, part, rows, cols = parts[0].shape
    tile = math.gcd(part, begin) if begin else part
    tile = math.gcd(tile, 2 * STEP)
    first = begin // tile
    here = pl.BlockSpec((1, tile, rows, cols), lambda i: (0, i, 0, 0))
    half = rows // 2
    shapes = [(feats, half, cols), (feats, half * fold, cols // fold)] if fold else [(feats, rows, cols)]
    return pl.pallas_call(
        functools.partial(settle_body, fold, len(parts)),
        grid=(part // tile,),
        in_specs=[here] * len(parts) + [pl.BlockSpec(memory_space=pl.ANY)] * len(before),
        out_specs=[pl.BlockSpec((tile,) + s[1:], lambda i: (first + i, 0, 0)) for s in shapes],
        out_shape=[jax.ShapeDtypeStruct(s, WIDE) for s in shapes],
        input_output_aliases={len(parts) + k: k for k in range(len(before))},
        cost_estimate=pl.CostEstimate(
            flops=4 * part * rows * cols, transcendentals=0, bytes_accessed=12 * part * rows * cols
        ),
        compiler_params=pltpu.CompilerParams(vmem_limit_bytes=6 * MIB),
        name="settle",
    )(*parts, *before)


def line_sum(keep, send, line):
    parts = [keep, lax.ppermute(send, "dp", [(i, i ^ 1) for i in range(CORES * line)])]
    for t in range(line.bit_length() - 1):
        half = line >> (t + 1)
        total = sum(a[half : 2 * half].astype(WIDE) for a in parts).astype(NARROW)
        hop = CORES << t
        parts.append(lax.ppermute(total, "dp", [(i, i ^ hop) for i in range(CORES * line)]))
    return parts


def is_joint(c, chunks):
    return c < chunks - 2


def local(tokens, first_up, second_up, first_down, second_down, cotangent):
    groups = lax.axis_size("block")
    line = lax.axis_size("dp") // CORES
    feats = second_up.shape[0]
    blocks = first_up.shape[0]
    chunks = split(feats)

    def exchange(arrays):
        got = [arrays[0]]
        for s in range(1, groups):
            got.append(lax.ppermute(arrays[s], "block", [(i, i ^ s) for i in range(groups)]))
        return got

    packed = mix_in(tokens, cotangent, first_up, second_down, groups)
    packed = [exchange(a) for a in packed]
    fold = second_up.shape[2] // second_up.shape[1]
    for_v, for_d, sums = [], [], []
    for c, (_, begin) in enumerate(chunks):
        joint = is_joint(c, len(chunks))
        back, keep, send = feature(packed[c], second_up, first_down, begin, joint, line)
        for_v.append(exchange(back[:groups]))
        for_d.append(for_v[-1] if joint else exchange(back[groups:]))
        sums.append(line_sum(keep, send, line))
    done = ()
    for c, (_, begin) in enumerate(chunks):
        done = settle(sums[c], fold, begin, feats, done)
    red_su, red_fd = done
    result, keep, send = mix_out(for_v, cotangent, second_down, True, line)
    sum_v = line_sum(keep, send, line)
    input_rows, keep, send = mix_out(for_d, tokens, first_up, False, line)
    sum_d = line_sum(keep, send, line)
    (red_sd,) = settle(sum_v, 0, 0, blocks, ())
    (red_fu,) = settle(sum_d, 0, 0, blocks, ())
    return (result, input_rows, red_fu, red_su, red_fd, red_sd)


def plain_local(tokens, first_up, second_up, first_down, second_down, cotangent):
    groups = lax.axis_size("block")
    blocks, width = first_up.shape[:2]
    feats = width // groups
    count = tokens.shape[0]
    x = tokens.reshape(count, blocks, width)
    g = cotangent.reshape(count, blocks, width)

    def mul(spec, a, b):
        return jnp.einsum(spec, a, b, preferred_element_type=WIDE)

    def to_feats(array):
        array = array.astype(NARROW).reshape(count, blocks, groups, feats).transpose(0, 2, 1, 3)
        array = lax.all_to_all(array, "block", split_axis=1, concat_axis=1, tiled=True)
        return array.reshape(count, -1, feats)

    def to_blocks(array):
        array = array.astype(NARROW).reshape(count, groups, blocks, feats)
        array = lax.all_to_all(array, "block", split_axis=1, concat_axis=1, tiled=True)
        return array.transpose(0, 2, 1, 3).reshape(count, blocks, width)

    u = to_feats(mul("tbi,bij->tbj", x, first_up))
    d = to_feats(mul("tbi,bji->tbj", g, second_down))
    active, slope = gelu_pair(mul("tbj,jbk->tjk", u, second_up))
    active = active.astype(NARROW)
    v = to_blocks(mul("tjk,jkb->tbj", active, first_down))
    back = (mul("tbj,jkb->tjk", d, first_down) * slope).astype(NARROW)
    e = to_blocks(mul("tjk,jbk->tbj", back, second_up))
    grads = (
        mul("tbi,tbj->bij", x, e),
        mul("tbj,tjk->jbk", u, back),
        mul("tjk,tbj->jkb", active, d),
        mul("tbj,tbi->bji", v, g),
    )
    result = mul("tbj,bji->tbi", v, second_down).astype(NARROW)
    input_rows = mul("tbj,bij->tbi", e, first_up).astype(NARROW)
    reduced = tuple(lax.psum_scatter(a, "dp", scatter_dimension=1, tiled=True) for a in grads)
    return (result.reshape(count, -1), input_rows.reshape(count, -1)) + reduced


def solution(mesh):
    placed = (
        P("dp", "block"),
        P("block", None, None),
        P("block", None, None),
        P("block", None, None),
        P("block", None, None),
        P("dp", "block"),
    )
    groups, n_dp = mesh.shape["block"], mesh.shape["dp"]
    line = n_dp // CORES

    def suits(first_up, second_up, tokens):
        blocks, width, _ = first_up.shape
        blocks = blocks // groups
        hidden = second_up.shape[2]
        return (
            groups & (groups - 1) == 0
            and n_dp % CORES == 0
            and line > 1
            and line & (line - 1) == 0
            and blocks % ROWS == 0
            and width % LANES == 0
            and hidden % width == 0
            and width % (n_dp * ROWS) == 0
            and tokens.shape[0] // n_dp % LANES == 0
        )

    def step(tokens, first_up, second_up, first_down, second_down, cotangent):
        fits = suits(first_up, second_up, tokens)

        def body(*args):
            return (local if fits else plain_local)(*args)

        run = jax.shard_map(
            body,
            mesh=mesh,
            in_specs=placed,
            out_specs=(
                P("dp", "block"),
                P("dp", "block"),
                P("block", "dp", None),
                P("block", "dp", None),
                P("block", "dp", None),
                P("block", "dp", None),
            ),
            check_vma=False,
        )
        return run(tokens, first_up, second_up, first_down, second_down, cotangent)

    return step
```

```python
import functools
import math

import jax
import jax.numpy as jnp
from jax import lax
from jax.experimental import pallas as pl
from jax.experimental.pallas import tpu as pltpu
from jax.sharding import PartitionSpec as P


NARROW = jnp.bfloat16
WIDE = jnp.float32
LANES = 128
ROWS = 16
PITCH = 20
SHARES = (2, 2, 2, 2)
TILE = 128
MIB = 1 << 20
STEP = 4
CORES = 2


def gelu_pair(values):
    factor = math.sqrt(2.0 / math.pi)
    square = values * values
    tanh_part = jnp.tanh(factor * values * (1.0 + 0.044715 * square))
    half = 0.5 + 0.5 * tanh_part
    active = values * half
    slope_term = half + active * (1.0 - tanh_part) * (factor + (3.0 * 0.044715 * factor) * square)
    return (active, slope_term)


def dot(a, b, ca, cb):
    return lax.dot_general(a, b, (((ca,), (cb,)), ((), ())), preferred_element_type=WIDE)


def spread(scr, b, width, value):
    for h in range(scr.shape[0]):
        scr[h, pl.ds(b, width, stride=PITCH), :] = value[:, h * LANES : (h + 1) * LANES]


def split(feats):
    unit, rest = divmod(feats, sum(SHARES))
    sizes = [feats] if rest else [unit * share for share in SHARES]
    return [(size, sum(sizes[:c])) for c, size in enumerate(sizes)]


def mix_in_body(groups, x_ref, g_ref, fu_ref, sd_ref, *rest):
    outs, (scr_u, scr_d) = rest[:-2], rest[-2:]
    rows, width = fu_ref.shape[0], fu_ref.shape[1]
    me = lax.axis_index("block")
    feats = width // groups
    for b in range(rows):
        cols = slice(b * width, (b + 1) * width)
        spread(scr_u, b, width, dot(fu_ref[b], x_ref[:, cols], 0, 1))
        spread(scr_d, b, width, dot(sd_ref[b], g_ref[:, cols], 1, 1))
    for c, (part, begin) in enumerate(split(feats)):
        for s in range(groups):
            ref = outs[c * groups + s]
            off = pl.multiple_of(((me ^ s) * feats + begin) * PITCH, 8)
            for k, scr in enumerate((scr_u, scr_d)):
                for h in range(scr.shape[0]):
                    for n in range(part):
                        value = scr[h, pl.ds(off + n * PITCH, rows), :]
                        ref[k, n, :, h * LANES : (h + 1) * LANES] = value.astype(NARROW)


def mix_in(tokens, cotangent, first_up, second_down, groups):
    count = tokens.shape[0]
    blocks, width = first_up.shape[:2]
    parts = [size for size, _ in split(width // groups)]
    flat = pl.BlockSpec((count, ROWS * width), lambda i: (0, i))
    mats = pl.BlockSpec((ROWS, width, width), lambda i: (i, 0, 0))
    outs = [pl.BlockSpec((2, n, ROWS, count), lambda i: (0, 0, i, 0)) for n in parts for _ in range(groups)]
    res = pl.pallas_call(
        functools.partial(mix_in_body, groups),
        grid=(blocks // ROWS,),
        in_specs=[flat, flat, mats, mats],
        out_specs=outs,
        scratch_shapes=[pltpu.VMEM((count // LANES, width * PITCH, LANES), WIDE)] * 2,
        out_shape=[
            jax.ShapeDtypeStruct((2, n, blocks, count), NARROW) for n in parts for _ in range(groups)
        ],
        cost_estimate=pl.CostEstimate(
            flops=4 * count * blocks * width * width, transcendentals=0, bytes_accessed=8 * count * blocks * width
        ),
        compiler_params=pltpu.CompilerParams(vmem_limit_bytes=24 * MIB),
        name="mix_in",
    )(tokens, cotangent, first_up, second_down)
    return [res[c * groups : (c + 1) * groups] for c in range(len(parts))]


def mirrored(value, bits):
    return sum(((value >> t) & 1) << (bits - 1 - t) for t in range(bits))


def line_slots(line):
    bits = line.bit_length() - 1
    own = mirrored(lax.axis_index("dp") // CORES, bits)
    return [own ^ mirrored(p, bits) for p in range(line)]


def feature_body(groups, line, *rest):
    ins, (wu_ref, wd_ref) = rest[:groups], rest[groups : groups + 2]
    outs = rest[groups + 2 : -8]
    keep_ref, send_ref, u_scr, d_scr, v_scr, e_scr, a_scr, b_scr = rest[-8:]
    me = lax.axis_index("block")
    first = lax.axis_index("dp") % CORES == 0
    blocks = ins[0].shape[2]
    offs = [pl.multiple_of((me ^ s) * blocks, ROWS) for s in range(groups)]
    slots = line_slots(line)
    for n in range(wu_ref.shape[0]):
        for s in range(groups):
            u_scr[n, pl.ds(offs[s], blocks), :] = ins[s][0, n]
            d_scr[n, pl.ds(offs[s], blocks), :] = ins[s][1, n]
    hidden = wd_ref.shape[1]
    for n in range(wu_ref.shape[0]):
        u, d = u_scr[n], d_scr[n]
        for k in range(0, hidden, TILE):
            tile = slice(k, k + TILE)
            active, slope = gelu_pair(dot(wu_ref[n, :, tile], u, 0, 0))
            a_scr[n, tile, :] = active.astype(NARROW)
            b_scr[n, tile, :] = (dot(wd_ref[n, tile, :], d, 1, 0) * slope).astype(NARROW)
    for n in range(wu_ref.shape[0]):
        u, d = u_scr[n], d_scr[n]
        active, back = a_scr[n], b_scr[n]
        v_scr[n] = dot(wd_ref[n], active, 0, 0).astype(NARROW)
        e_scr[n] = dot(wu_ref[n], back, 1, 0).astype(NARROW)
        g_su = dot(u, back, 1, 1).astype(NARROW)
        g_fd = dot(active, d, 1, 1).astype(NARROW)
        r_su = g_su.shape[0] // (CORES * line)
        r_fd = g_fd.shape[0] // (CORES * line)
        fold = g_su.shape[1] // g_fd.shape[1]
        step = r_fd // fold
        for p, at in enumerate(slots):
            halves = []
            for k in range(CORES):
                r = p * CORES + k
                block = g_fd[r * r_fd : (r + 1) * r_fd]
                wide = jnp.concatenate([block[f * step : (f + 1) * step] for f in range(fold)], axis=1)
                halves.append((g_su[r * r_su : (r + 1) * r_su], wide))
            for h in range(2):
                rows = slice(h * r_su, (h + 1) * r_su)
                keep_ref[at, n, rows, :] = jnp.where(first, halves[0][h], halves[1][h])
                send_ref[at, n, rows, :] = jnp.where(first, halves[1][h], halves[0][h])
    for n in range(wu_ref.shape[0]):
        for s in range(groups):
            outs[s][0, n] = v_scr[n, pl.ds(offs[s], blocks), :]
            outs[len(outs) - groups + s][outs[0].shape[0] - 1, n] = e_scr[n, pl.ds(offs[s], blocks), :]


def feature(arrays, second_up, first_down, begin, joint, line):
    groups = len(arrays)
    _, part, blocks, count = arrays[0].shape
    width, hidden = second_up.shape[1:]
    r_su = width // (CORES * line)
    each = math.gcd(STEP, part, begin)
    first = begin // each
    steps = part // each
    kinds = 2 if joint else 1
    n_out = 2 * groups // kinds
    back = pl.BlockSpec((kinds, each, blocks, count), lambda i: (0, i, 0, 0))
    data = pl.BlockSpec((2, each, blocks, count), lambda i: (0, i, 0, 0))
    grads = pl.BlockSpec((line, each, 2 * r_su, hidden), lambda i: (0, i, 0, 0))
    g_shape = jax.ShapeDtypeStruct((line, part, 2 * r_su, hidden), NARROW)
    scr = pltpu.VMEM((each, groups * blocks, count), NARROW)
    res = pl.pallas_call(
        functools.partial(feature_body, groups, line),
        grid=(steps,),
        in_specs=[data] * groups
        + [
            pl.BlockSpec((each, width, hidden), lambda i: (first + i, 0, 0)),
            pl.BlockSpec((each, hidden, width), lambda i: (first + i, 0, 0)),
        ],
        out_specs=[back] * n_out + [grads] * 2,
        scratch_shapes=[scr] * 4 + [pltpu.VMEM((each, hidden, count), NARROW)] * 2,
        out_shape=[jax.ShapeDtypeStruct((kinds, part, blocks, count), NARROW)] * n_out + [g_shape] * 2,
        cost_estimate=pl.CostEstimate(
            flops=12 * part * count * width * hidden,
            transcendentals=part * count * hidden,
            bytes_accessed=part * (8 * width * hidden + 8 * count * width),
        ),
        compiler_params=pltpu.CompilerParams(vmem_limit_bytes=20 * MIB),
        name="feature",
    )(*arrays, second_up, first_down)
    return res[:-2], res[-2], res[-1]


def mix_out_body(groups, line, to_output, *rest):
    ins = rest[:-6]
    flat_ref, mats_ref, out_ref, keep_ref, send_ref, scr = rest[-6:]
    rows, width = mats_ref.shape[0], mats_ref.shape[1]
    me = lax.axis_index("block")
    first = lax.axis_index("dp") % CORES == 0
    slots = line_slots(line)
    feats = width // groups
    for c, (part, begin) in enumerate(split(feats)):
        for s in range(groups):
            ref = ins[c * groups + s]
            off = pl.multiple_of(((me ^ s) * feats + begin) * PITCH, 8)
            for h in range(scr.shape[0]):
                for n in range(part):
                    value = ref[0, n, :, h * LANES : (h + 1) * LANES]
                    scr[h, pl.ds(off + n * PITCH, rows), :] = value.astype(WIDE)
    r_one = width // (CORES * line)
    for b in range(rows):
        cols = slice(b * width, (b + 1) * width)
        pieces = [scr[h, pl.ds(b, width, stride=PITCH), :] for h in range(scr.shape[0])]
        y = jnp.concatenate(pieces, axis=1).astype(NARROW)
        if to_output:
            out_ref[:, cols] = dot(y, mats_ref[b], 0, 0).astype(NARROW)
            grad = dot(y, flat_ref[:, cols], 1, 0).astype(NARROW)
        else:
            out_ref[:, cols] = dot(y, mats_ref[b], 0, 1).astype(NARROW)
            grad = dot(flat_ref[:, cols], y, 0, 1).astype(NARROW)
        for p, at in enumerate(slots):
            halves = [grad[(p * CORES + k) * r_one : (p * CORES + k + 1) * r_one] for k in range(CORES)]
            keep_ref[at, b] = jnp.where(first, halves[0], halves[1])
            send_ref[at, b] = jnp.where(first, halves[1], halves[0])


def mix_out(arrays, flat_in, mats_in, to_output, line):
    groups = len(arrays[0])
    blocks, width = mats_in.shape[:2]
    count = flat_in.shape[0]
    r_one = width // (CORES * line)

    def data(array):
        kind = 0 if to_output or array.shape[0] == 1 else 1
        return pl.BlockSpec((1, array.shape[1], ROWS, count), lambda i: (kind, 0, i, 0))

    flat = pl.BlockSpec((count, ROWS * width), lambda i: (0, i))
    mats = pl.BlockSpec((ROWS, width, width), lambda i: (i, 0, 0))
    grads = pl.BlockSpec((line, ROWS, r_one, width), lambda i: (0, i, 0, 0))
    g_shape = jax.ShapeDtypeStruct((line, blocks, r_one, width), NARROW)
    pieces = [a for chunk in arrays for a in chunk]
    return pl.pallas_call(
        functools.partial(mix_out_body, groups, line, to_output),
        grid=(blocks // ROWS,),
        in_specs=[data(a) for a in pieces] + [flat, mats],
        out_specs=[flat, grads, grads],
        scratch_shapes=[pltpu.VMEM((count // LANES, width * PITCH, LANES), WIDE)],
        out_shape=[jax.ShapeDtypeStruct(flat_in.shape, NARROW), g_shape, g_shape],
        cost_estimate=pl.CostEstimate(
            flops=4 * count * blocks * width * width, transcendentals=0, bytes_accessed=8 * count * blocks * width
        ),
        compiler_params=pltpu.CompilerParams(vmem_limit_bytes=18 * MIB),
        name="mix_out",
    )(*pieces, flat_in, mats_in)


def settle_body(fold, n_sum, *rest):
    ins, first_ref = rest[:n_sum], rest[-2 if fold else -1]
    total = ins[0][0].astype(WIDE)
    for ref in ins[1:]:
        total = total + ref[0].astype(WIDE)
    half = first_ref.shape[1]
    first_ref[...] = total[:, :half]
    for f in range(fold):
        second_ref = rest[-1]
        width = second_ref.shape[2]
        second_ref[:, f * half : (f + 1) * half, :] = total[:, half:, f * width : (f + 1) * width]


def settle(parts, fold, begin, feats, before):
    _, part, rows, cols = parts[0].shape
    tile = math.gcd(part, begin) if begin else part
    tile = math.gcd(tile, 2 * STEP)
    first = begin // tile
    here = pl.BlockSpec((1, tile, rows, cols), lambda i: (0, i, 0, 0))
    half = rows // 2
    shapes = [(feats, half, cols), (feats, half * fold, cols // fold)] if fold else [(feats, rows, cols)]
    return pl.pallas_call(
        functools.partial(settle_body, fold, len(parts)),
        grid=(part // tile,),
        in_specs=[here] * len(parts) + [pl.BlockSpec(memory_space=pl.ANY)] * len(before),
        out_specs=[pl.BlockSpec((tile,) + s[1:], lambda i: (first + i, 0, 0)) for s in shapes],
        out_shape=[jax.ShapeDtypeStruct(s, WIDE) for s in shapes],
        input_output_aliases={len(parts) + k: k for k in range(len(before))},
        cost_estimate=pl.CostEstimate(
            flops=4 * part * rows * cols, transcendentals=0, bytes_accessed=12 * part * rows * cols
        ),
        compiler_params=pltpu.CompilerParams(vmem_limit_bytes=6 * MIB),
        name="settle",
    )(*parts, *before)


def line_sum(keep, send, line):
    parts = [keep, lax.ppermute(send, "dp", [(i, i ^ 1) for i in range(CORES * line)])]
    for t in range(line.bit_length() - 1):
        half = line >> (t + 1)
        total = sum(a[half : 2 * half].astype(WIDE) for a in parts).astype(NARROW)
        hop = CORES << t
        parts.append(lax.ppermute(total, "dp", [(i, i ^ hop) for i in range(CORES * line)]))
    return parts


def is_joint(c, chunks):
    return c < chunks - 2


def local(tokens, first_up, second_up, first_down, second_down, cotangent):
    groups = lax.axis_size("block")
    line = lax.axis_size("dp") // CORES
    feats = second_up.shape[0]
    blocks = first_up.shape[0]
    chunks = split(feats)

    def exchange(arrays):
        got = [arrays[0]]
        for s in range(1, groups):
            got.append(lax.ppermute(arrays[s], "block", [(i, i ^ s) for i in range(groups)]))
        return got

    first_in = [pltpu.with_memory_space_constraint(a, pltpu.HBM) for a in (tokens, cotangent, first_up, second_down)]
    packed = mix_in(*first_in, groups)
    packed = [exchange(a) for a in packed]
    fold = second_up.shape[2] // second_up.shape[1]
    for_v, for_d, sums = [], [], []
    for c, (_, begin) in enumerate(chunks):
        joint = is_joint(c, len(chunks))
        back, keep, send = feature(packed[c], second_up, first_down, begin, joint, line)
        for_v.append(exchange(back[:groups]))
        for_d.append(for_v[-1] if joint else exchange(back[groups:]))
        sums.append(line_sum(keep, send, line))
    done = ()
    for c, (_, begin) in enumerate(chunks):
        done = settle(sums[c], fold, begin, feats, done)
    red_su, red_fd = done
    result, keep, send = mix_out(for_v, cotangent, second_down, True, line)
    sum_v = line_sum(keep, send, line)
    input_rows, keep, send = mix_out(for_d, tokens, first_up, False, line)
    sum_d = line_sum(keep, send, line)
    (red_sd,) = settle(sum_v, 0, 0, blocks, ())
    (red_fu,) = settle(sum_d, 0, 0, blocks, ())
    return (result, input_rows, red_fu, red_su, red_fd, red_sd)


def plain_local(tokens, first_up, second_up, first_down, second_down, cotangent):
    groups = lax.axis_size("block")
    blocks, width = first_up.shape[:2]
    feats = width // groups
    count = tokens.shape[0]
    x = tokens.reshape(count, blocks, width)
    g = cotangent.reshape(count, blocks, width)

    def mul(spec, a, b):
        return jnp.einsum(spec, a, b, preferred_element_type=WIDE)

    def to_feats(array):
        array = array.astype(NARROW).reshape(count, blocks, groups, feats).transpose(0, 2, 1, 3)
        array = lax.all_to_all(array, "block", split_axis=1, concat_axis=1, tiled=True)
        return array.reshape(count, -1, feats)

    def to_blocks(array):
        array = array.astype(NARROW).reshape(count, groups, blocks, feats)
        array = lax.all_to_all(array, "block", split_axis=1, concat_axis=1, tiled=True)
        return array.transpose(0, 2, 1, 3).reshape(count, blocks, width)

    u = to_feats(mul("tbi,bij->tbj", x, first_up))
    d = to_feats(mul("tbi,bji->tbj", g, second_down))
    active, slope = gelu_pair(mul("tbj,jbk->tjk", u, second_up))
    active = active.astype(NARROW)
    v = to_blocks(mul("tjk,jkb->tbj", active, first_down))
    back = (mul("tbj,jkb->tjk", d, first_down) * slope).astype(NARROW)
    e = to_blocks(mul("tjk,jbk->tbj", back, second_up))
    grads = (
        mul("tbi,tbj->bij", x, e),
        mul("tbj,tjk->jbk", u, back),
        mul("tjk,tbj->jkb", active, d),
        mul("tbj,tbi->bji", v, g),
    )
    result = mul("tbj,bji->tbi", v, second_down).astype(NARROW)
    input_rows = mul("tbj,bij->tbi", e, first_up).astype(NARROW)
    reduced = tuple(lax.psum_scatter(a, "dp", scatter_dimension=1, tiled=True) for a in grads)
    return (result.reshape(count, -1), input_rows.reshape(count, -1)) + reduced


def solution(mesh):
    placed = (
        P("dp", "block"),
        P("block", None, None),
        P("block", None, None),
        P("block", None, None),
        P("block", None, None),
        P("dp", "block"),
    )
    groups, n_dp = mesh.shape["block"], mesh.shape["dp"]
    line = n_dp // CORES

    def suits(first_up, second_up, tokens):
        blocks, width, _ = first_up.shape
        blocks = blocks // groups
        hidden = second_up.shape[2]
        return (
            groups & (groups - 1) == 0
            and n_dp % CORES == 0
            and line > 1
            and line & (line - 1) == 0
            and blocks % ROWS == 0
            and width % LANES == 0
            and width // groups % sum(SHARES) == 0
            and hidden % width == 0
            and width % (n_dp * ROWS) == 0
            and tokens.shape[0] // n_dp % LANES == 0
        )

    def step(tokens, first_up, second_up, first_down, second_down, cotangent):
        fits = suits(first_up, second_up, tokens)

        def body(*args):
            return (local if fits else plain_local)(*args)

        run = jax.shard_map(
            body,
            mesh=mesh,
            in_specs=placed,
            out_specs=(
                P("dp", "block"),
                P("dp", "block"),
                P("block", "dp", None),
                P("block", "dp", None),
                P("block", "dp", None),
                P("block", "dp", None),
            ),
            check_vma=False,
        )
        return run(tokens, first_up, second_up, first_down, second_down, cotangent)

    return step
```

```python
import functools
import math

import jax
import jax.numpy as jnp
from jax import lax
from jax.experimental import pallas as pl
from jax.experimental.pallas import tpu as pltpu
from jax.sharding import PartitionSpec as P


NARROW = jnp.bfloat16
WIDE = jnp.float32
LANES = 128
ROWS = 16
PITCH = 20
SHARES = (1, 2, 2, 2, 1)
TILE = 128
MIB = 1 << 20
STEP = 4
CORES = 2


def gelu_pair(values):
    factor = math.sqrt(2.0 / math.pi)
    square = values * values
    tanh_part = jnp.tanh(factor * values * (1.0 + 0.044715 * square))
    half = 0.5 + 0.5 * tanh_part
    active = values * half
    slope_term = half + active * (1.0 - tanh_part) * (factor + (3.0 * 0.044715 * factor) * square)
    return (active, slope_term)


def dot(a, b, ca, cb):
    return lax.dot_general(a, b, (((ca,), (cb,)), ((), ())), preferred_element_type=WIDE)


def spread(scr, b, width, value):
    for h in range(scr.shape[0]):
        scr[h, pl.ds(b, width, stride=PITCH), :] = value[:, h * LANES : (h + 1) * LANES]


def split(feats):
    unit, rest = divmod(feats, sum(SHARES))
    sizes = [feats] if rest else [unit * share for share in SHARES]
    return [(size, sum(sizes[:c])) for c, size in enumerate(sizes)]


def mix_in_body(groups, x_ref, g_ref, fu_ref, sd_ref, *rest):
    outs, (scr_u, scr_d) = rest[:-2], rest[-2:]
    rows, width = fu_ref.shape[0], fu_ref.shape[1]
    me = lax.axis_index("block")
    feats = width // groups
    for b in range(rows):
        cols = slice(b * width, (b + 1) * width)
        spread(scr_u, b, width, dot(fu_ref[b], x_ref[:, cols], 0, 1))
        spread(scr_d, b, width, dot(sd_ref[b], g_ref[:, cols], 1, 1))
    for c, (part, begin) in enumerate(split(feats)):
        for s in range(groups):
            ref = outs[c * groups + s]
            off = pl.multiple_of(((me ^ s) * feats + begin) * PITCH, 8)
            for k, scr in enumerate((scr_u, scr_d)):
                for h in range(scr.shape[0]):
                    for n in range(part):
                        value = scr[h, pl.ds(off + n * PITCH, rows), :]
                        ref[k, n, :, h * LANES : (h + 1) * LANES] = value.astype(NARROW)


def mix_in(tokens, cotangent, first_up, second_down, groups):
    count = tokens.shape[0]
    blocks, width = first_up.shape[:2]
    parts = [size for size, _ in split(width // groups)]
    flat = pl.BlockSpec((count, ROWS * width), lambda i: (0, i))
    mats = pl.BlockSpec((ROWS, width, width), lambda i: (i, 0, 0))
    outs = [pl.BlockSpec((2, n, ROWS, count), lambda i: (0, 0, i, 0)) for n in parts for _ in range(groups)]
    res = pl.pallas_call(
        functools.partial(mix_in_body, groups),
        grid=(blocks // ROWS,),
        in_specs=[flat, flat, mats, mats],
        out_specs=outs,
        scratch_shapes=[pltpu.VMEM((count // LANES, width * PITCH, LANES), WIDE)] * 2,
        out_shape=[
            jax.ShapeDtypeStruct((2, n, blocks, count), NARROW) for n in parts for _ in range(groups)
        ],
        cost_estimate=pl.CostEstimate(
            flops=4 * count * blocks * width * width, transcendentals=0, bytes_accessed=8 * count * blocks * width
        ),
        compiler_params=pltpu.CompilerParams(vmem_limit_bytes=24 * MIB),
        name="mix_in",
    )(tokens, cotangent, first_up, second_down)
    return [res[c * groups : (c + 1) * groups] for c in range(len(parts))]


def mirrored(value, bits):
    return sum(((value >> t) & 1) << (bits - 1 - t) for t in range(bits))


def line_slots(line):
    bits = line.bit_length() - 1
    own = mirrored(lax.axis_index("dp") // CORES, bits)
    return [own ^ mirrored(p, bits) for p in range(line)]


def feature_body(groups, line, *rest):
    ins, (wu_ref, wd_ref) = rest[:groups], rest[groups : groups + 2]
    outs = rest[groups + 2 : -8]
    keep_ref, send_ref, u_scr, d_scr, v_scr, e_scr, a_scr, b_scr = rest[-8:]
    me = lax.axis_index("block")
    first = lax.axis_index("dp") % CORES == 0
    blocks = ins[0].shape[2]
    offs = [pl.multiple_of((me ^ s) * blocks, ROWS) for s in range(groups)]
    slots = line_slots(line)
    for n in range(wu_ref.shape[0]):
        for s in range(groups):
            u_scr[n, pl.ds(offs[s], blocks), :] = ins[s][0, n]
            d_scr[n, pl.ds(offs[s], blocks), :] = ins[s][1, n]
    hidden = wd_ref.shape[1]
    for n in range(wu_ref.shape[0]):
        u, d = u_scr[n], d_scr[n]
        for k in range(0, hidden, TILE):
            tile = slice(k, k + TILE)
            active, slope = gelu_pair(dot(wu_ref[n, :, tile], u, 0, 0))
            a_scr[n, tile, :] = active.astype(NARROW)
            b_scr[n, tile, :] = (dot(wd_ref[n, tile, :], d, 1, 0) * slope).astype(NARROW)
    for n in range(wu_ref.shape[0]):
        u, d = u_scr[n], d_scr[n]
        active, back = a_scr[n], b_scr[n]
        v_scr[n] = dot(wd_ref[n], active, 0, 0).astype(NARROW)
        e_scr[n] = dot(wu_ref[n], back, 1, 0).astype(NARROW)
        g_su = dot(u, back, 1, 1).astype(NARROW)
        g_fd = dot(active, d, 1, 1).astype(NARROW)
        r_su = g_su.shape[0] // (CORES * line)
        r_fd = g_fd.shape[0] // (CORES * line)
        fold = g_su.shape[1] // g_fd.shape[1]
        step = r_fd // fold
        for p, at in enumerate(slots):
            halves = []
            for k in range(CORES):
                r = p * CORES + k
                block = g_fd[r * r_fd : (r + 1) * r_fd]
                wide = jnp.concatenate([block[f * step : (f + 1) * step] for f in range(fold)], axis=1)
                halves.append((g_su[r * r_su : (r + 1) * r_su], wide))
            for h in range(2):
                rows = slice(h * r_su, (h + 1) * r_su)
                keep_ref[at, n, rows, :] = jnp.where(first, halves[0][h], halves[1][h])
                send_ref[at, n, rows, :] = jnp.where(first, halves[1][h], halves[0][h])
    for n in range(wu_ref.shape[0]):
        for s in range(groups):
            outs[s][0, n] = v_scr[n, pl.ds(offs[s], blocks), :]
            outs[len(outs) - groups + s][outs[0].shape[0] - 1, n] = e_scr[n, pl.ds(offs[s], blocks), :]


def feature(arrays, second_up, first_down, begin, joint, line):
    groups = len(arrays)
    _, part, blocks, count = arrays[0].shape
    width, hidden = second_up.shape[1:]
    r_su = width // (CORES * line)
    each = math.gcd(STEP, part, begin)
    first = begin // each
    steps = part // each
    kinds = 2 if joint else 1
    n_out = 2 * groups // kinds
    back = pl.BlockSpec((kinds, each, blocks, count), lambda i: (0, i, 0, 0))
    data = pl.BlockSpec((2, each, blocks, count), lambda i: (0, i, 0, 0))
    grads = pl.BlockSpec((line, each, 2 * r_su, hidden), lambda i: (0, i, 0, 0))
    g_shape = jax.ShapeDtypeStruct((line, part, 2 * r_su, hidden), NARROW)
    scr = pltpu.VMEM((each, groups * blocks, count), NARROW)
    res = pl.pallas_call(
        functools.partial(feature_body, groups, line),
        grid=(steps,),
        in_specs=[data] * groups
        + [
            pl.BlockSpec((each, width, hidden), lambda i: (first + i, 0, 0)),
            pl.BlockSpec((each, hidden, width), lambda i: (first + i, 0, 0)),
        ],
        out_specs=[back] * n_out + [grads] * 2,
        scratch_shapes=[scr] * 4 + [pltpu.VMEM((each, hidden, count), NARROW)] * 2,
        out_shape=[jax.ShapeDtypeStruct((kinds, part, blocks, count), NARROW)] * n_out + [g_shape] * 2,
        cost_estimate=pl.CostEstimate(
            flops=12 * part * count * width * hidden,
            transcendentals=part * count * hidden,
            bytes_accessed=part * (8 * width * hidden + 8 * count * width),
        ),
        compiler_params=pltpu.CompilerParams(vmem_limit_bytes=20 * MIB),
        name="feature",
    )(*arrays, second_up, first_down)
    return res[:-2], res[-2], res[-1]


def mix_out_body(groups, line, to_output, *rest):
    ins = rest[:-6]
    flat_ref, mats_ref, out_ref, keep_ref, send_ref, scr = rest[-6:]
    rows, width = mats_ref.shape[0], mats_ref.shape[1]
    me = lax.axis_index("block")
    first = lax.axis_index("dp") % CORES == 0
    slots = line_slots(line)
    feats = width // groups
    for c, (part, begin) in enumerate(split(feats)):
        for s in range(groups):
            ref = ins[c * groups + s]
            off = pl.multiple_of(((me ^ s) * feats + begin) * PITCH, 8)
            for h in range(scr.shape[0]):
                for n in range(part):
                    value = ref[0, n, :, h * LANES : (h + 1) * LANES]
                    scr[h, pl.ds(off + n * PITCH, rows), :] = value.astype(WIDE)
    r_one = width // (CORES * line)
    for b in range(rows):
        cols = slice(b * width, (b + 1) * width)
        pieces = [scr[h, pl.ds(b, width, stride=PITCH), :] for h in range(scr.shape[0])]
        y = jnp.concatenate(pieces, axis=1).astype(NARROW)
        if to_output:
            out_ref[:, cols] = dot(y, mats_ref[b], 0, 0).astype(NARROW)
            grad = dot(y, flat_ref[:, cols], 1, 0).astype(NARROW)
        else:
            out_ref[:, cols] = dot(y, mats_ref[b], 0, 1).astype(NARROW)
            grad = dot(flat_ref[:, cols], y, 0, 1).astype(NARROW)
        for p, at in enumerate(slots):
            halves = [grad[(p * CORES + k) * r_one : (p * CORES + k + 1) * r_one] for k in range(CORES)]
            keep_ref[at, b] = jnp.where(first, halves[0], halves[1])
            send_ref[at, b] = jnp.where(first, halves[1], halves[0])


def mix_out(arrays, flat_in, mats_in, to_output, line):
    groups = len(arrays[0])
    blocks, width = mats_in.shape[:2]
    count = flat_in.shape[0]
    r_one = width // (CORES * line)

    def data(array):
        kind = 0 if to_output or array.shape[0] == 1 else 1
        return pl.BlockSpec((1, array.shape[1], ROWS, count), lambda i: (kind, 0, i, 0))

    flat = pl.BlockSpec((count, ROWS * width), lambda i: (0, i))
    mats = pl.BlockSpec((ROWS, width, width), lambda i: (i, 0, 0))
    grads = pl.BlockSpec((line, ROWS, r_one, width), lambda i: (0, i, 0, 0))
    g_shape = jax.ShapeDtypeStruct((line, blocks, r_one, width), NARROW)
    pieces = [a for chunk in arrays for a in chunk]
    return pl.pallas_call(
        functools.partial(mix_out_body, groups, line, to_output),
        grid=(blocks // ROWS,),
        in_specs=[data(a) for a in pieces] + [flat, mats],
        out_specs=[flat, grads, grads],
        scratch_shapes=[pltpu.VMEM((count // LANES, width * PITCH, LANES), WIDE)],
        out_shape=[jax.ShapeDtypeStruct(flat_in.shape, NARROW), g_shape, g_shape],
        cost_estimate=pl.CostEstimate(
            flops=4 * count * blocks * width * width, transcendentals=0, bytes_accessed=8 * count * blocks * width
        ),
        compiler_params=pltpu.CompilerParams(vmem_limit_bytes=18 * MIB),
        name="mix_out",
    )(*pieces, flat_in, mats_in)


def settle_body(fold, n_sum, *rest):
    ins, first_ref = rest[:n_sum], rest[-2 if fold else -1]
    total = ins[0][0].astype(WIDE)
    for ref in ins[1:]:
        total = total + ref[0].astype(WIDE)
    half = first_ref.shape[1]
    first_ref[...] = total[:, :half]
    for f in range(fold):
        second_ref = rest[-1]
        width = second_ref.shape[2]
        second_ref[:, f * half : (f + 1) * half, :] = total[:, half:, f * width : (f + 1) * width]


def settle(parts, fold, begin, feats, before):
    _, part, rows, cols = parts[0].shape
    tile = math.gcd(part, begin) if begin else part
    tile = math.gcd(tile, 2 * STEP)
    first = begin // tile
    here = pl.BlockSpec((1, tile, rows, cols), lambda i: (0, i, 0, 0))
    half = rows // 2
    shapes = [(feats, half, cols), (feats, half * fold, cols // fold)] if fold else [(feats, rows, cols)]
    return pl.pallas_call(
        functools.partial(settle_body, fold, len(parts)),
        grid=(part // tile,),
        in_specs=[here] * len(parts) + [pl.BlockSpec(memory_space=pl.ANY)] * len(before),
        out_specs=[pl.BlockSpec((tile,) + s[1:], lambda i: (first + i, 0, 0)) for s in shapes],
        out_shape=[jax.ShapeDtypeStruct(s, WIDE) for s in shapes],
        input_output_aliases={len(parts) + k: k for k in range(len(before))},
        cost_estimate=pl.CostEstimate(
            flops=4 * part * rows * cols, transcendentals=0, bytes_accessed=12 * part * rows * cols
        ),
        compiler_params=pltpu.CompilerParams(vmem_limit_bytes=6 * MIB),
        name="settle",
    )(*parts, *before)


def line_sum(keep, send, line):
    parts = [keep, lax.ppermute(send, "dp", [(i, i ^ 1) for i in range(CORES * line)])]
    for t in range(line.bit_length() - 1):
        half = line >> (t + 1)
        total = sum(a[half : 2 * half].astype(WIDE) for a in parts).astype(NARROW)
        hop = CORES << t
        parts.append(lax.ppermute(total, "dp", [(i, i ^ hop) for i in range(CORES * line)]))
    return parts


def is_joint(c, chunks):
    return c < chunks - 2


def local(tokens, first_up, second_up, first_down, second_down, cotangent):
    groups = lax.axis_size("block")
    line = lax.axis_size("dp") // CORES
    feats = second_up.shape[0]
    blocks = first_up.shape[0]
    chunks = split(feats)

    def exchange(arrays):
        got = [arrays[0]]
        for s in range(1, groups):
            got.append(lax.ppermute(arrays[s], "block", [(i, i ^ s) for i in range(groups)]))
        return got

    factors = [pltpu.with_memory_space_constraint(a, pltpu.HBM) for a in (second_up, first_down)]
    first_in = [pltpu.with_memory_space_constraint(a, pltpu.HBM) for a in (tokens, cotangent, first_up, second_down)]
    packed = mix_in(*first_in, groups)
    packed = [exchange(a) for a in packed]
    fold = second_up.shape[2] // second_up.shape[1]
    for_v, for_d, sums = [], [], []
    for c, (_, begin) in enumerate(chunks):
        joint = is_joint(c, len(chunks))
        mats = factors if c == 0 else (second_up, first_down)
        back, keep, send = feature(packed[c], *mats, begin, joint, line)
        for_v.append(exchange(back[:groups]))
        for_d.append(for_v[-1] if joint else exchange(back[groups:]))
        sums.append(line_sum(keep, send, line))
    done = ()
    for c, (_, begin) in enumerate(chunks):
        done = settle(sums[c], fold, begin, feats, done)
    red_su, red_fd = done
    result, keep, send = mix_out(for_v, cotangent, second_down, True, line)
    sum_v = line_sum(keep, send, line)
    input_rows, keep, send = mix_out(for_d, tokens, first_up, False, line)
    sum_d = line_sum(keep, send, line)
    (red_sd,) = settle(sum_v, 0, 0, blocks, ())
    (red_fu,) = settle(sum_d, 0, 0, blocks, ())
    return (result, input_rows, red_fu, red_su, red_fd, red_sd)


def plain_local(tokens, first_up, second_up, first_down, second_down, cotangent):
    groups = lax.axis_size("block")
    blocks, width = first_up.shape[:2]
    feats = width // groups
    count = tokens.shape[0]
    x = tokens.reshape(count, blocks, width)
    g = cotangent.reshape(count, blocks, width)

    def mul(spec, a, b):
        return jnp.einsum(spec, a, b, preferred_element_type=WIDE)

    def to_feats(array):
        array = array.astype(NARROW).reshape(count, blocks, groups, feats).transpose(0, 2, 1, 3)
        array = lax.all_to_all(array, "block", split_axis=1, concat_axis=1, tiled=True)
        return array.reshape(count, -1, feats)

    def to_blocks(array):
        array = array.astype(NARROW).reshape(count, groups, blocks, feats)
        array = lax.all_to_all(array, "block", split_axis=1, concat_axis=1, tiled=True)
        return array.transpose(0, 2, 1, 3).reshape(count, blocks, width)

    u = to_feats(mul("tbi,bij->tbj", x, first_up))
    d = to_feats(mul("tbi,bji->tbj", g, second_down))
    active, slope = gelu_pair(mul("tbj,jbk->tjk", u, second_up))
    active = active.astype(NARROW)
    v = to_blocks(mul("tjk,jkb->tbj", active, first_down))
    back = (mul("tbj,jkb->tjk", d, first_down) * slope).astype(NARROW)
    e = to_blocks(mul("tjk,jbk->tbj", back, second_up))
    grads = (
        mul("tbi,tbj->bij", x, e),
        mul("tbj,tjk->jbk", u, back),
        mul("tjk,tbj->jkb", active, d),
        mul("tbj,tbi->bji", v, g),
    )
    result = mul("tbj,bji->tbi", v, second_down).astype(NARROW)
    input_rows = mul("tbj,bij->tbi", e, first_up).astype(NARROW)
    reduced = tuple(lax.psum_scatter(a, "dp", scatter_dimension=1, tiled=True) for a in grads)
    return (result.reshape(count, -1), input_rows.reshape(count, -1)) + reduced


def solution(mesh):
    placed = (
        P("dp", "block"),
        P("block", None, None),
        P("block", None, None),
        P("block", None, None),
        P("block", None, None),
        P("dp", "block"),
    )
    groups, n_dp = mesh.shape["block"], mesh.shape["dp"]
    line = n_dp // CORES

    def suits(first_up, second_up, tokens):
        blocks, width, _ = first_up.shape
        blocks = blocks // groups
        hidden = second_up.shape[2]
        return (
            groups & (groups - 1) == 0
            and n_dp % CORES == 0
            and line > 1
            and line & (line - 1) == 0
            and blocks % ROWS == 0
            and width % LANES == 0
            and width // groups % sum(SHARES) == 0
            and hidden % width == 0
            and width % (n_dp * ROWS) == 0
            and tokens.shape[0] // n_dp % LANES == 0
        )

    def step(tokens, first_up, second_up, first_down, second_down, cotangent):
        fits = suits(first_up, second_up, tokens)

        def body(*args):
            return (local if fits else plain_local)(*args)

        run = jax.shard_map(
            body,
            mesh=mesh,
            in_specs=placed,
            out_specs=(
                P("dp", "block"),
                P("dp", "block"),
                P("block", "dp", None),
                P("block", "dp", None),
                P("block", "dp", None),
                P("block", "dp", None),
            ),
            check_vma=False,
        )
        return run(tokens, first_up, second_up, first_down, second_down, cotangent)

    return step
```
